128 devices in a mesh: tok: 16 (over z, x_hi, core), ch: 8 (over y, x_lo).
Axes of the slice: x: 4 (x_hi: 2, x_lo: 2; x = x_hi * 2 + x_lo), y: 4, z: 4, core: 2. Of those that a mesh axis runs over, the one named last changes fastest.
Arguments:
- activations: bfloat16 [2048, 8192], P('ch', 'tok'), may hold values from -6 to 6
- proj_weight: bfloat16 [8192, 24576], P('tok', 'ch'), may hold values from -0.0625 to 0.0625
- short_taps: float32 [3, 3, 8192], replicated, may hold values from -3.5 to 3.5
- residues: float32 [16, 8192], replicated, may hold values from -0.25 to 0.25
- decay_rates: float32 [16, 8192], replicated, may hold values from 0.00012207031 to 0.1
- skip_gain: float32 [8192], replicated, may hold values from 0.5 to 1.5
- out_weight: bfloat16 [8192, 8192], P('ch', 'tok'), may hold values from -0.0625 to 0.0625
Outputs:
- layer_out: bfloat16 [2048, 8192], P('ch', 'tok')
The draws below stay inside these ranges and needn't reach their ends.
All inputs are finite; a program needn't handle non-finite values.
Results may differ from the reference program's by a relative error of at most 0.035.
Values may be sent and summed in bfloat16 or wider, within the bound.
No kernel may reach another device: no remote copies, remote signals or barrier semaphores. Data moves between devices by JAX's collectives and lax.ppermute only.
A program may use at most 192 MiB of HBM per device.

```python
import math
import jax
import jax.numpy as jnp
from jax import lax

D = 8192
SEQ = 2048
GROUP = 64
TAPS = 3
ORDER = 16
FEAT_BLOCK = 512
OUT_BLOCK = 1024


def block_scale(stream_key, shape, shards, least, largest):
    loudness = 1.0
    for dim, parts in shards:
        heights = jax.random.uniform(jax.random.fold_in(jax.random.fold_in(stream_key, 6), dim), (parts,), jnp.float32, least / len(shards), largest / len(shards))
        loudness = loudness * jnp.repeat(jnp.exp(heights), shape[dim] // parts).reshape((-1,) + (1,) * (len(shape) - 1 - dim))
    return loudness


def noise(own_key, extent, spread, most, cuts=(), held_as=jnp.bfloat16):
    values = jax.random.normal(own_key, extent, jnp.float32) * spread
    if len(cuts) > 0:
        values = block_scale(own_key, extent, cuts, -0.22, 0.18) * values
    return jnp.clip(values, min=-most, max=most).astype(held_as)


def setup_inputs(seed: int = 0) -> dict:
    streams_of = jax.random.split(jax.random.key(seed), 8)
    return {
        "activations": noise(streams_of[0], (SEQ, D), 1.0, 6.0, ((0, 8), (1, 16))),
        "proj_weight": noise(streams_of[1], (D, 3 * D), D ** -0.5, 0.0625, ((0, 16), (1, 8))),
        "short_taps": noise(streams_of[2], (3, TAPS, D), TAPS ** -0.5, 3.5, (), jnp.float32),
        "residues": noise(streams_of[3], (ORDER, D), (3.0 / (ORDER * SEQ) ** 0.5), 0.25, (), jnp.float32),
        "decay_rates": jnp.clip(jnp.exp(jax.random.uniform(streams_of[4], (ORDER, D), jnp.float32, math.log(0.00012207031), math.log(0.1))), 0.00012207031, 0.1),
        "skip_gain": jnp.clip(jax.random.uniform(streams_of[5], (D,), jnp.float32, 0.5, 1.5), 0.5, 1.5),
        "out_weight": noise(streams_of[6], (D, D), D ** -0.5, 0.0625, ((0, 8), (1, 16))),
    }


def blocked_product(left_mat, right_mat, width):
    running = jnp.zeros((left_mat.shape[0], right_mat.shape[1]), jnp.float32)
    for first in range(0, left_mat.shape[1], width):
        partial_prod = jnp.dot(left_mat[:, first:first + width], right_mat[first:first + width], preferred_element_type=jnp.float32)
        rounded = lax.optimization_barrier(partial_prod.astype(jnp.bfloat16))
        running = running + rounded.astype(jnp.float32)
    return running.astype(jnp.bfloat16)


def featurize(column, tap_rows):
    values = column.astype(jnp.float32)
    padded = jnp.pad(values, ((TAPS - 1, 0), (0, 0)))
    result = jnp.zeros_like(values)
    for offset in range(TAPS):
        begin = TAPS - 1 - offset
        result = result + tap_rows[offset] * padded[begin:begin + SEQ]
    return result


def reference(activations, proj_weight, short_taps, residues, decay_rates, skip_gain, out_weight):
    projected = blocked_product(activations, proj_weight, FEAT_BLOCK)
    grouped = projected.reshape(SEQ, D // GROUP, 3, GROUP)
    queries = featurize(grouped[:, :, 0, :].reshape(SEQ, D), short_taps[0])
    key_feat = featurize(grouped[:, :, 1, :].reshape(SEQ, D), short_taps[1])
    value_feat = featurize(grouped[:, :, 2, :].reshape(SEQ, D), short_taps[2])
    gate_input = key_feat * value_feat
    positions = jnp.arange(SEQ).astype(jnp.float32)[:, None]
    kernel = jnp.zeros((SEQ, D), jnp.float32)
    for term_index in range(ORDER):
        kernel = kernel + residues[term_index] * jnp.exp(-decay_rates[term_index] * positions)
    length_total = 2 * SEQ
    spectrum = jnp.fft.rfft(gate_input, n=length_total, axis=0) * jnp.fft.rfft(kernel, n=length_total, axis=0)
    convolved = jnp.fft.irfft(spectrum, n=length_total, axis=0)[:SEQ] + skip_gain * gate_input
    gated = (queries * convolved).astype(jnp.bfloat16)
    return blocked_product(gated, out_weight, OUT_BLOCK)
```

```python
import math

import jax
import jax.numpy as jnp
from jax import lax
from jax.experimental import pallas as pl
from jax.experimental.pallas import tpu as pltpu
from jax.sharding import PartitionSpec as P

GROUP = 64
Z, XH, CORES = 4, 2, 2
Y, XL = 4, 2
BF = jnp.bfloat16
F32 = jnp.float32


EXACT_PRODUCT = lax.Precision.HIGHEST


def tok_perm(move):
    pairs = []
    for z in range(Z):
        for xh in range(XH):
            for c in range(CORES):
                nz, nx, nc = move(z, xh, c)
                pairs.append(((z * XH + xh) * CORES + c, ((nz % Z) * XH + nx) * CORES + nc))
    return pairs


def ch_perm(move):
    pairs = []
    for y in range(Y):
        for xl in range(XL):
            ny, nx = move(y, xl)
            pairs.append((y * XL + xl, (ny % Y) * XL + nx))
    return pairs


CORE_SWAP = tok_perm(lambda z, xh, c: (z, xh, 1 - c))
Z_UP = tok_perm(lambda z, xh, c: (z + 1, xh, c))
Z_DOWN = tok_perm(lambda z, xh, c: (z - 1, xh, c))
X_SWAP = tok_perm(lambda z, xh, c: (z, 1 - xh, c))
XL_SWAP = ch_perm(lambda y, xl: (y, 1 - xl))


def tok_send(value, perm):
    return lax.ppermute(value, "tok", perm)


def ch_send(value, perm):
    return lax.ppermute(value, "ch", perm)


def weight_kernel(where_ref, weight_ref, keep_ref, send_ref, turned):
    turned[...] = weight_ref[...].T
    width = keep_ref.shape[0]
    core = where_ref[2]
    keep_ref[...] = turned[pl.ds(pl.multiple_of(core * width, width), width), :]
    send_ref[...] = turned[pl.ds(pl.multiple_of((1 - core) * width, width), width), :]


def split_weight(proj_weight, where):
    depth, cols = proj_weight.shape
    width = cols // (Z * XH * CORES)
    steps = Z * XH

    def source(g, where_ref):
        return (0, ((where_ref[0] + g // XH) % Z) * XH + (where_ref[1] + g) % XH)

    shape = jax.ShapeDtypeStruct((steps * width, depth), BF)
    return pl.pallas_call(
        weight_kernel,
        out_shape=(shape, shape),
        grid_spec=pltpu.PrefetchScalarGridSpec(
            num_scalar_prefetch=1,
            grid=(steps,),
            in_specs=[pl.BlockSpec((depth, CORES * width), source)],
            out_specs=[pl.BlockSpec((width, depth), lambda g, w: (g, 0))] * 2,
            scratch_shapes=[pltpu.VMEM((CORES * width, depth), BF)],
        ),
        name="split_weight",
    )(where, proj_weight)


def add(*terms):
    total = terms[0].astype(F32)
    for term in terms[1:]:
        total = total + term.astype(F32)
    return total.astype(BF)


def ring_sum(part):
    from_below = tok_send(part(2, 0), Z_UP)
    from_above = tok_send(part(2, 1), Z_DOWN)
    below_b = tok_send(part(1, 1), Z_UP)
    above_a = tok_send(part(3, 0), Z_DOWN)
    below_a = tok_send(add(part(1, 0), from_below), Z_UP)
    above_b = tok_send(add(part(3, 1), from_above), Z_DOWN)
    return add(part(0, 0), below_a, above_a), add(part(0, 1), below_b, above_b)


def nt_dot(left, right):
    return lax.dot_general(left, right, (((1,), (1,)), ((), ())), preferred_element_type=F32)


def project(rows, weights, width):
    own = {}
    for dz in range(Z):
        for half in range(XH):
            first = (dz * XH + half) * width
            own[dz, half] = nt_dot(weights[first : first + width], rows).astype(BF)
    near, far = ring_sum(lambda dz, half: own[dz, half])
    return add(near, tok_send(far, X_SWAP))


def phase_table(row_count, col_count, period):
    row_ids = lax.broadcasted_iota(jnp.int32, (row_count, col_count), 0)
    col_ids = lax.broadcasted_iota(jnp.int32, (row_count, col_count), 1)
    angles = (row_ids * col_ids % period).astype(jnp.float32) * (-2.0 * math.pi / period)
    return (jnp.cos(angles), jnp.sin(angles))


def forward_transform(signal, tables):
    cos_rows, sin_rows, cos_twist, sin_twist, cos_cols, sin_cols = tables
    chan_count = signal.shape[0]
    shaped = signal.reshape(chan_count, cos_rows.shape[0], cos_cols.shape[0])
    step_real = jnp.einsum("ka,cab->ckb", cos_rows, shaped, precision=EXACT_PRODUCT)
    step_imag = jnp.einsum("ka,cab->ckb", sin_rows, shaped, precision=EXACT_PRODUCT)
    turn_real = step_real * cos_twist - step_imag * sin_twist
    turn_imag = step_real * sin_twist + step_imag * cos_twist
    spec_real = jnp.einsum(
        "ckb,bm->ckm", turn_real, cos_cols, precision=EXACT_PRODUCT
    ) - jnp.einsum("ckb,bm->ckm", turn_imag, sin_cols, precision=EXACT_PRODUCT)
    spec_imag = jnp.einsum(
        "ckb,bm->ckm", turn_real, sin_cols, precision=EXACT_PRODUCT
    ) + jnp.einsum("ckb,bm->ckm", turn_imag, cos_cols, precision=EXACT_PRODUCT)
    return (spec_real, spec_imag)


def inverse_transform(spec_real, spec_imag, tables):
    cos_rows, sin_rows, cos_twist, sin_twist, cos_cols, sin_cols = tables
    step_real = jnp.einsum(
        "ckm,mb->ckb", spec_real, cos_cols, precision=EXACT_PRODUCT
    ) + jnp.einsum("ckm,mb->ckb", spec_imag, sin_cols, precision=EXACT_PRODUCT)
    step_imag = jnp.einsum(
        "ckm,mb->ckb", spec_imag, cos_cols, precision=EXACT_PRODUCT
    ) - jnp.einsum("ckm,mb->ckb", spec_real, sin_cols, precision=EXACT_PRODUCT)
    turn_real = step_real * cos_twist + step_imag * sin_twist
    turn_imag = step_imag * cos_twist - step_real * sin_twist
    restored = jnp.einsum("nk,ckb->cnb", cos_rows, turn_real, precision=EXACT_PRODUCT) + jnp.einsum(
        "nk,ckb->cnb", sin_rows, turn_imag, precision=EXACT_PRODUCT
    )
    length_total = cos_rows.shape[0] * cos_cols.shape[0]
    return restored.reshape(restored.shape[0], length_total) / float(length_total)


def long_gate(projected, tap_slice, chan_res, chan_rates, chan_skip):
    chan_dev = projected.shape[0] // 3
    seq_len = projected.shape[1]
    grouped = projected.reshape(3, chan_dev, seq_len)
    tap_count = tap_slice.shape[1]

    def featurize(component):
        values = grouped[component].astype(jnp.float32)
        padded = jnp.pad(values, ((0, 0), (tap_count - 1, 0)))
        result = jnp.zeros_like(values)
        for offset in range(tap_count):
            begin = tap_count - 1 - offset
            result = (
                result + tap_slice[component, offset][:, None] * padded[:, begin : begin + seq_len]
            )
        return result

    queries = featurize(0)
    gate_input = featurize(1) * featurize(2)
    positions = lax.iota(jnp.float32, seq_len)[None, :]
    kernel = jnp.zeros((chan_dev, seq_len), jnp.float32)
    for term_index in range(chan_res.shape[0]):
        kernel = kernel + chan_res[term_index][:, None] * jnp.exp(
            -chan_rates[term_index][:, None] * positions
        )
    length_total = 2 * seq_len
    col_count = min(128, length_total)
    row_count = length_total // col_count
    cos_rows, sin_rows = phase_table(row_count, row_count, row_count)
    cos_twist, sin_twist = phase_table(row_count, col_count, length_total)
    cos_cols, sin_cols = phase_table(col_count, col_count, col_count)
    tables = (cos_rows, sin_rows, cos_twist, sin_twist, cos_cols, sin_cols)
    padding = ((0, 0), (0, seq_len))
    gate_real, gate_imag = forward_transform(jnp.pad(gate_input, padding), tables)
    kern_real, kern_imag = forward_transform(jnp.pad(kernel, padding), tables)
    prod_real = gate_real * kern_real - gate_imag * kern_imag
    prod_imag = gate_real * kern_imag + gate_imag * kern_real
    convolved = (
        inverse_transform(prod_real, prod_imag, tables)[:, :seq_len]
        + chan_skip[:, None] * gate_input
    )
    return (queries * convolved).astype(jnp.bfloat16)


def body(activations, proj_weight, short_taps, residues, decay_rates, skip_gain, out_weight):
    tok_index = lax.axis_index("tok")
    ch_index = lax.axis_index("ch")
    z, xh, core = tok_index // (XH * CORES), tok_index // CORES % XH, tok_index % CORES
    y, xl = ch_index // XL, ch_index % XL
    where = jnp.stack([z, xh, core]).astype(jnp.int32)
    block_rows = activations.shape[0]
    width = proj_weight.shape[1] // (Z * XH * CORES)
    chan_dev = width // 3
    blocks = Y * XL

    across = ch_send(activations, XL_SWAP)
    groups = []
    for mine in (activations, across):
        pieces = [mine]
        for dy in range(1, Y):
            pieces.append(ch_send(mine, ch_perm(lambda y, xl, dy=dy: (y - dy, xl))))
        groups.append(jnp.concatenate(pieces, axis=0))

    keep, give = split_weight(proj_weight, where)
    weights = jnp.concatenate([keep, tok_send(give, CORE_SWAP)], axis=1)

    projected_groups = []
    for rows in groups:
        both = jnp.concatenate([rows, tok_send(rows, CORE_SWAP)], axis=1)
        projected_groups.append(project(both, weights, width))
    relative = jnp.concatenate(projected_groups, axis=1)

    def relative_of(ay, ax):
        return (ax + xl) % XL * Y + (ay - y) % Y

    ordered = jnp.concatenate(
        [
            lax.dynamic_slice_in_dim(relative, relative_of(b // XL, b % XL) * block_rows, block_rows, 1)
            for b in range(blocks)
        ],
        axis=1,
    )

    start_chan = (ch_index * lax.axis_size("tok") + tok_index) * chan_dev
    gated = long_gate(
        ordered,
        lax.dynamic_slice_in_dim(short_taps, start_chan, chan_dev, 2),
        lax.dynamic_slice_in_dim(residues, start_chan, chan_dev, 1),
        lax.dynamic_slice_in_dim(decay_rates, start_chan, chan_dev, 1),
        lax.dynamic_slice_in_dim(skip_gain, start_chan, chan_dev, 0),
    )

    pieces = []
    for dz in range(Z):
        for dx in range(XH):
            if dz == 0 and dx == 0:
                pieces.append(gated)
            else:
                pieces.append(
                    tok_send(gated, tok_perm(lambda z, xh, c, dz=dz, dx=dx: (z - dz, xh ^ dx, c)))
                )
    same_core = jnp.concatenate(pieces, axis=0)
    gathered = jnp.concatenate([same_core, tok_send(same_core, CORE_SWAP)], axis=0)
    shaped = out_weight.reshape(Z, XH, CORES, chan_dev, out_weight.shape[1])
    out_pieces = []
    for dc in range(CORES):
        for dz in range(Z):
            for dx in range(XH):
                index = ((z + dz) % Z, (xh + dx) % XH, (core + dc) % CORES, 0, 0)
                out_pieces.append(
                    lax.dynamic_slice(shaped, index, (1, 1, 1) + shaped.shape[3:]).reshape(
                        shaped.shape[3:]
                    )
                )
    out_rows = jnp.concatenate(out_pieces, axis=0)

    partial = lax.dot_general(
        gathered, out_rows, (((0,), (0,)), ((), ())), preferred_element_type=F32
    ).astype(BF)
    terms = []
    for dx in range(XL):
        for dy in range(Y):
            target = ((y + dy) % Y) * XL + (xl + dx) % XL
            term = lax.dynamic_slice_in_dim(partial, target * block_rows, block_rows, 0)
            if dx or dy:
                term = ch_send(term, ch_perm(lambda y, xl, dx=dx, dy=dy: (y + dy, xl ^ dx)))
            terms.append(term)
    return add(*terms)


def solution(mesh):
    return jax.shard_map(
        body,
        mesh=mesh,
        in_specs=(P("ch", "tok"), P("tok", "ch"), P(), P(), P(), P(), P("ch", "tok")),
        out_specs=P("ch", "tok"),
        check_vma=False,
    )
```

```python
import jax
import jax.numpy as jnp
from jax import lax
from jax.experimental import pallas as pl
from jax.experimental.pallas import tpu as pltpu
from jax.sharding import PartitionSpec as P

Z, XH, CORES = 4, 2, 2
Y, XL = 4, 2
BLOCKS = Y * XL
LANES = 128
BF = jnp.bfloat16
F32 = jnp.float32


def tok_perm(move):
    pairs = []
    for z in range(Z):
        for xh in range(XH):
            for c in range(CORES):
                nz, nx, nc = move(z, xh, c)
                pairs.append(((z * XH + xh) * CORES + c, ((nz % Z) * XH + nx) * CORES + nc))
    return pairs


def ch_perm(move):
    pairs = []
    for y in range(Y):
        for xl in range(XL):
            ny, nx = move(y, xl)
            pairs.append((y * XL + xl, (ny % Y) * XL + nx))
    return pairs


CORE_SWAP = tok_perm(lambda z, xh, c: (z, xh, 1 - c))
Z_UP = tok_perm(lambda z, xh, c: (z + 1, xh, c))
Z_DOWN = tok_perm(lambda z, xh, c: (z - 1, xh, c))
X_SWAP = tok_perm(lambda z, xh, c: (z, 1 - xh, c))


def tok_send(value, perm):
    return lax.ppermute(value, "tok", perm)


def ch_send(value, perm):
    return lax.ppermute(value, "ch", perm)


def swap(value):
    return tok_send(value, CORE_SWAP)


def add(*terms):
    total = terms[0].astype(F32)
    for term in terms[1:]:
        total = total + term.astype(F32)
    return total.astype(BF)


def whole(shape):
    return pl.BlockSpec(shape, lambda *_: (0,) * len(shape))


def project_kernel(pieces, targets, where_ref, *refs):
    rows_refs, (own_ref, other_ref), out_refs = (
        refs[:pieces],
        refs[pieces : pieces + 2],
        refs[pieces + 2 :],
    )
    rows = jnp.concatenate([ref[...] for ref in rows_refs], axis=0)
    depth = own_ref.shape[0]
    product = jnp.dot(rows[:, :depth], own_ref[...], preferred_element_type=F32) + jnp.dot(
        rows[:, depth:], other_ref[...], preferred_element_type=F32
    )
    product = product.astype(BF)
    for target in range(targets):

        @pl.when(pl.program_id(0) == target)
        def _(target=target):
            out_refs[target][...] = product


def project(pieces, own_weight, other_weight, where, steps):
    depth, cols = own_weight.shape
    width = cols // (Z * XH)
    tokens = sum(piece.shape[0] for piece in pieces)
    targets = len(steps) * XH

    def source(g, where_ref):
        step = steps[0]
        for k in range(1, len(steps)):
            step = jnp.where(g // XH == k, steps[k], step)
        return (0, ((where_ref[0] + step) % Z) * XH + (where_ref[1] + g) % XH)

    outs = pl.pallas_call(
        lambda *refs: project_kernel(len(pieces), targets, *refs),
        out_shape=[jax.ShapeDtypeStruct((tokens, width), BF)] * targets,
        grid_spec=pltpu.PrefetchScalarGridSpec(
            num_scalar_prefetch=1,
            grid=(targets,),
            in_specs=[whole(piece.shape) for piece in pieces]
            + [pl.BlockSpec((depth, width), source)] * 2,
            out_specs=[whole((tokens, width))] * targets,
        ),
        cost_estimate=pl.CostEstimate(
            flops=2 * tokens * 2 * depth * width * targets,
            bytes_accessed=2 * (tokens * 2 * depth + 2 * depth * width * targets + tokens * width * targets),
            transcendentals=0,
        ),
        name="project",
    )(where, *pieces, own_weight, other_weight)
    return {(steps[k // XH], k % XH): outs[k] for k in range(targets)}


def reduce_chips(pieces, own_weight, other_weight, where):
    part = project(pieces, own_weight, other_weight, where, (2,))
    from_below = tok_send(part[2, 0], Z_UP)
    from_above = tok_send(part[2, 1], Z_DOWN)
    part.update(project(pieces, own_weight, other_weight, where, (1, 3)))
    far_below = tok_send(part[1, 1], Z_UP)
    near_above = tok_send(part[3, 0], Z_DOWN)
    part.update(project(pieces, own_weight, other_weight, where, (0,)))
    far_above = tok_send(add(part[3, 1], from_above), Z_DOWN)
    near_below = tok_send(add(part[1, 0], from_below), Z_UP)
    across = tok_send(add(part[0, 1], far_below, far_above), X_SWAP)
    return [part[0, 0], near_above, near_below, across]


def features(block):
    half = LANES // 2
    low = lax.broadcasted_iota(jnp.int32, (1, LANES), 1) < half
    first, second, third = (block[:, k * LANES : (k + 1) * LANES] for k in range(3))
    return (
        jnp.where(low, first, second),
        jnp.where(low, pltpu.roll(first, half, 1), pltpu.roll(third, half, 1)),
        jnp.where(low, second, third),
    )


def every(ref, row, length):
    return ref[pl.ds(row, BLOCKS, stride=length), :]


def local_kernel(groups, where_ref, taps_ref, rates_ref, *refs):
    count = 4
    term_refs = [refs[g * count : (g + 1) * count] for g in range(groups)]
    query_ref, gate_ref, edge_ref = refs[groups * count : groups * count + 3]
    raw_refs = refs[groups * count + 3 : groups * count + 6]
    key_ref, value_ref = refs[groups * count + 6 :]
    length = gate_ref.shape[0] // BLOCKS
    order = rates_ref.shape[0]
    rows = lax.broadcasted_iota(jnp.int32, (length, LANES), 0)
    for g in range(groups):
        for dy in range(Y):
            here = slice(dy * length, (dy + 1) * length)
            block = term_refs[g][0][here, :].astype(F32)
            for ref in term_refs[g][1:]:
                block = block + ref[here, :].astype(F32)
            spot = (lax.rem(where_ref[3] + dy, Y)) * XL + lax.rem(where_ref[4] + g, XL)
            there = pl.ds(pl.multiple_of(spot * length, length), length)
            mixed = []
            for f, raw in enumerate(features(block)):
                raw_refs[f][there, :] = raw
                total = taps_ref[3 * f : 3 * f + 1, :] * raw
                for back in (1, 2):
                    moved = jnp.where(rows >= back, pltpu.roll(raw, back, 0), 0.0)
                    total = total + taps_ref[3 * f + back : 3 * f + back + 1, :] * moved
                mixed.append(total)
            query_ref[there, :] = mixed[0]
            key_ref[there, :] = mixed[1]
            value_ref[there, :] = mixed[2]
            gate_ref[there, :] = mixed[1] * mixed[2]
    decay = [
        jnp.broadcast_to(jnp.exp(-rates_ref[n : n + 1, :]), (BLOCKS, LANES)) for n in range(order)
    ]

    def step(r, states):
        gate = every(gate_ref, r, length)
        return tuple(decay[n] * states[n] + gate for n in range(order))

    states = lax.fori_loop(
        2, length, step, tuple(jnp.zeros((BLOCKS, LANES), F32) for _ in range(order)), unroll=6
    )
    for n in range(order):
        edge_ref[n] = states[n]
    at = order
    for r in (0, 1):
        edge_ref[at] = every(key_ref, r, length)
        edge_ref[at + 1] = every(value_ref, r, length)
        at += 2
    for f in range(3):
        for r in (length - 1, length - 2):
            edge_ref[at] = every(raw_refs[f], r, length)
            at += 1


def filter_kernel(where_ref, taps_ref, rates_ref, weights_ref, skip_ref, mine_ref, theirs_ref, query_ref, gate_ref, out_ref, work):
    length = gate_ref.shape[0] // BLOCKS
    order = rates_ref.shape[0]
    core = where_ref[2]
    first = core == 0
    spots = lax.broadcasted_iota(jnp.int32, (BLOCKS, LANES), 0)

    def later(value, count):
        return jnp.where(spots >= count, pltpu.roll(value, count, 0), 0.0)

    def tap(f, back):
        return taps_ref[3 * f + back : 3 * f + back + 1, :]

    def head(ref, before_ref, is_first):
        def before(f, back):
            value = before_ref[order + 4 + 2 * f + back - 1]
            return jnp.where(is_first, later(value, 1), value)

        key0 = ref[order] + tap(1, 1) * before(1, 1) + tap(1, 2) * before(1, 2)
        value0 = ref[order + 1] + tap(2, 1) * before(2, 1) + tap(2, 2) * before(2, 2)
        key1 = ref[order + 2] + tap(1, 2) * before(1, 1)
        value1 = ref[order + 3] + tap(2, 2) * before(2, 1)
        query0 = tap(0, 1) * before(0, 1) + tap(0, 2) * before(0, 2)
        query1 = tap(0, 2) * before(0, 1)
        return key0 * value0, key1 * value1, query0, query1

    gate0, gate1, query0, query1 = head(mine_ref, theirs_ref, first)
    their0, their1, _, _ = head(theirs_ref, mine_ref, jnp.logical_not(first))
    decay, states = [], []
    for n in range(order):
        rate = rates_ref[n : n + 1, :]
        factor0, factor1 = jnp.exp(-(length - 1) * rate), jnp.exp(-(length - 2) * rate)
        ours = mine_ref[n] + factor0 * gate0 + factor1 * gate1
        theirs = theirs_ref[n] + factor0 * their0 + factor1 * their1
        early, late = jnp.where(first, ours, theirs), jnp.where(first, theirs, ours)
        half = jnp.exp(-length * rate)
        total = half * early + late
        for count in (1, 2, 4):
            total = total + jnp.exp(-(2 * length * count) * rate) * later(total, count)
        before = later(total, 1)
        states.append(jnp.where(first, before, half * before + early))
        decay.append(jnp.broadcast_to(jnp.exp(-rate), (BLOCKS, LANES)))
    weights = [jnp.broadcast_to(weights_ref[n : n + 1, :], (BLOCKS, LANES)) for n in range(order)]
    skip = jnp.broadcast_to(skip_ref[...], (BLOCKS, LANES))

    def advance(r, states, gate, query):
        states = tuple(decay[n] * states[n] + gate for n in range(order))
        terms = [weights[n] * states[n] for n in range(order)] + [skip * gate]
        while len(terms) > 1:
            terms = [a + b for a, b in zip(terms[::2], terms[1::2])] + terms[len(terms) // 2 * 2 :]
        work[pl.ds(r, BLOCKS, stride=length), :] = query * terms[0]
        return states

    states = advance(0, tuple(states), gate0, every(query_ref, 0, length) + query0)
    states = advance(1, states, gate1, every(query_ref, 1, length) + query1)
    lax.fori_loop(
        2,
        length,
        lambda r, states: advance(r, states, every(gate_ref, r, length), every(query_ref, r, length)),
        states,
        unroll=6,
    )
    for g in range(XL):
        for dy in range(Y):
            spot = (lax.rem(where_ref[3] + dy, Y)) * XL + lax.rem(where_ref[4] + g, XL)
            there = pl.ds(pl.multiple_of(spot * length, length), length)
            place = (g * Y + dy) * length
            out_ref[place : place + length, :] = work[there, :].astype(BF)


def local_part(where, taps, rates, groups):
    tokens = sum(terms[0].shape[0] for terms in groups)
    flat = [term for terms in groups for term in terms]
    edges = rates.shape[0] + 10
    tall = jax.ShapeDtypeStruct((tokens, LANES), F32)
    return pl.pallas_call(
        lambda *refs: local_kernel(len(groups), *refs),
        out_shape=(tall, tall, jax.ShapeDtypeStruct((edges, BLOCKS, LANES), F32)),
        in_specs=[pl.BlockSpec(memory_space=pltpu.SMEM)]
        + [pl.BlockSpec(memory_space=pltpu.VMEM)] * (2 + len(flat)),
        out_specs=[pl.BlockSpec(memory_space=pltpu.VMEM)] * 3,
        scratch_shapes=[pltpu.VMEM((tokens, LANES), F32)] * 5,
        name="local_part",
    )(where, taps, rates, *flat)


def filtered(where, taps, rates, weights, skip, mine, theirs, query, gate):
    vmem = pl.BlockSpec(memory_space=pltpu.VMEM)
    return pl.pallas_call(
        filter_kernel,
        out_shape=jax.ShapeDtypeStruct(gate.shape, BF),
        in_specs=[pl.BlockSpec(memory_space=pltpu.SMEM)] + [vmem] * 8,
        out_specs=vmem,
        scratch_shapes=[pltpu.VMEM(gate.shape, F32)],
        name="filtered",
    )(where, taps, rates, weights, skip, mine, theirs, query, gate)


def output_kernel(count, where_ref, *refs):
    piece_refs, (own_ref, other_ref), out_refs = refs[:count], refs[count : count + 2], refs[count + 2 :]
    cols = own_ref.shape[1]
    swapped = where_ref[2] == 1
    rows = out_refs[0].shape[0]

    def weight(k):
        chip = lax.rem(where_ref[0] + k // XH, Z) * XH + lax.rem(where_ref[1] + k, XH)
        return pl.ds(pl.multiple_of(chip * LANES, LANES), LANES)

    for k in range(0, count, 2):
        left = jnp.concatenate([piece_refs[k][...], piece_refs[k + 1][...]], axis=1)
        for side, ref in enumerate((own_ref, other_ref)):
            right = jnp.concatenate([ref[weight(k), :], ref[weight(k + 1), :]], axis=0)
            product = jnp.dot(left, right, preferred_element_type=F32)
            acc = refs[-1]
            if k == 0:
                acc[side] = product
            else:
                acc[side] += product
    for d, out_ref in enumerate(out_refs[:-1]):
        for side in range(2):
            out_ref[:, side * cols : (side + 1) * cols] = acc[side, d * rows : (d + 1) * rows, :].astype(BF)


def output_parts(where, pieces, own_weight, other_weight):
    tokens = pieces[0].shape[0]
    cols = own_weight.shape[1]
    vmem = pl.BlockSpec(memory_space=pltpu.VMEM)
    return pl.pallas_call(
        lambda *refs: output_kernel(len(pieces), *refs),
        out_shape=[jax.ShapeDtypeStruct((tokens // BLOCKS, 2 * cols), BF)] * BLOCKS,
        in_specs=[pl.BlockSpec(memory_space=pltpu.SMEM)] + [vmem] * (len(pieces) + 2),
        out_specs=[vmem] * BLOCKS,
        scratch_shapes=[pltpu.VMEM((2, tokens, cols), F32)],
        name="output_parts",
    )(where, *pieces, own_weight, other_weight)


def body(activations, proj_weight, short_taps, residues, decay_rates, skip_gain, out_weight):
    tok_index = lax.axis_index("tok")
    ch_index = lax.axis_index("ch")
    z, xh, core = tok_index // (XH * CORES), tok_index // CORES % XH, tok_index % CORES
    y, xl = ch_index // XL, ch_index % XL
    where = jnp.stack([z, xh, core, y, xl]).astype(jnp.int32)
    length = activations.shape[0] // CORES

    kept = lax.dynamic_slice_in_dim(activations, core * length, length, 0)
    other = swap(lax.dynamic_slice_in_dim(activations, (1 - core) * length, length, 0))
    mine = jnp.concatenate([kept, other], axis=1)
    other_weight = swap(proj_weight)
    other_out = swap(out_weight)

    start = (ch_index * (Z * XH) + z * XH + xh) * LANES
    taps = lax.dynamic_slice_in_dim(short_taps, start, LANES, 2).reshape(-1, LANES)
    weights = lax.dynamic_slice_in_dim(residues, start, LANES, 1)
    rates = lax.dynamic_slice_in_dim(decay_rates, start, LANES, 1)
    skip = lax.dynamic_slice_in_dim(skip_gain, start, LANES, 0)[None]

    groups = []
    for dx in range(XL):
        pieces = []
        for dy in range(Y):
            if dx or dy:
                pieces.append(ch_send(mine, ch_perm(lambda y, xl, dx=dx, dy=dy: (y - dy, xl ^ dx))))
            else:
                pieces.append(mine)
        groups.append(reduce_chips(pieces, proj_weight, other_weight, where))
    query, gate, edges = local_part(where, taps, rates, groups)
    gated = filtered(where, taps, rates, weights, skip, edges, swap(edges), query, gate)

    pieces = [gated]
    for k in range(1, Z * XH):
        dz, dx = k // XH, k % XH
        pieces.append(tok_send(gated, tok_perm(lambda z, xh, c, dz=dz, dx=dx: (z - dz, xh ^ dx, c))))
    parts = output_parts(where, pieces, out_weight, other_out)
    terms = [parts[0]]
    for k in range(1, BLOCKS):
        dx, dy = k // Y, k % Y
        terms.append(ch_send(parts[k], ch_perm(lambda y, xl, dx=dx, dy=dy: (y + dy, xl ^ dx))))
    total = add(*terms)
    cols = out_weight.shape[1]
    kept, other = total[:, :cols], swap(total[:, cols:])
    return jnp.where(core == 0, jnp.concatenate([kept, other]), jnp.concatenate([other, kept]))


def solution(mesh):
    return jax.shard_map(
        body,
        mesh=mesh,
        in_specs=(P("ch", "tok"), P("tok", "ch"), P(), P(), P(), P(), P("ch", "tok")),
        out_specs=P("ch", "tok"),
        check_vma=False,
    )
```

```python
import jax
import jax.numpy as jnp
from jax import lax
from jax.experimental import pallas as pl
from jax.experimental.pallas import tpu as pltpu
from jax.sharding import PartitionSpec as P

Z, XH, CORES = 4, 2, 2
Y, XL = 4, 2
BLOCKS = Y * XL
LANES = 128
BF = jnp.bfloat16
F32 = jnp.float32


def tok_perm(move):
    pairs = []
    for z in range(Z):
        for xh in range(XH):
            for c in range(CORES):
                nz, nx, nc = move(z, xh, c)
                pairs.append(((z * XH + xh) * CORES + c, ((nz % Z) * XH + nx) * CORES + nc))
    return pairs


def ch_perm(move):
    pairs = []
    for y in range(Y):
        for xl in range(XL):
            ny, nx = move(y, xl)
            pairs.append((y * XL + xl, (ny % Y) * XL + nx))
    return pairs


CORE_SWAP = tok_perm(lambda z, xh, c: (z, xh, 1 - c))
Z_UP = tok_perm(lambda z, xh, c: (z + 1, xh, c))
Z_DOWN = tok_perm(lambda z, xh, c: (z - 1, xh, c))
X_SWAP = tok_perm(lambda z, xh, c: (z, 1 - xh, c))


def tok_send(value, perm):
    return lax.ppermute(value, "tok", perm)


def ch_send(value, perm):
    return lax.ppermute(value, "ch", perm)


def swap(value):
    return tok_send(value, CORE_SWAP)


def add(*terms):
    total = terms[0].astype(F32)
    for term in terms[1:]:
        total = total + term.astype(F32)
    return total.astype(BF)


def whole(shape):
    return pl.BlockSpec(shape, lambda *_: (0,) * len(shape))


TARGETS = [(2, 0), (1, 1), (2, 1), (3, 0), (1, 0), (0, 0), (0, 1), (3, 1)]


def chip_of(where_ref, dz, dx):
    return ((where_ref[0] + dz) & (Z - 1)) * XH + ((where_ref[1] + dx) & (XH - 1))


def reorder_kernel(targets, axis, where_ref, in_ref, out_ref, sems):
    size = in_ref.shape[axis] // len(targets)
    copies = []
    for k, (dz, dx) in enumerate(targets):
        source = pl.ds(pl.multiple_of(chip_of(where_ref, dz, dx) * size, size), size)
        place = pl.ds(k * size, size)
        if axis == 0:
            pair = in_ref.at[source, :], out_ref.at[place, :]
        else:
            pair = in_ref.at[:, source], out_ref.at[:, place]
        copies.append(pltpu.make_async_copy(*pair, sems.at[k]))
        copies[-1].start()
    for copy in copies:
        copy.wait()


def by_target(weight, where, targets, axis):
    return pl.pallas_call(
        lambda *refs: reorder_kernel(targets, axis, *refs),
        out_shape=jax.ShapeDtypeStruct(weight.shape, weight.dtype),
        in_specs=[pl.BlockSpec(memory_space=pltpu.SMEM), pl.BlockSpec(memory_space=pl.ANY)],
        out_specs=pl.BlockSpec(memory_space=pltpu.VMEM),
        scratch_shapes=[pltpu.SemaphoreType.DMA((len(targets),))],
        name="by_target",
    )(where, weight)


def product(rows, weights, first, last):
    depth, cols = weights[0].shape
    width = cols // len(TARGETS)
    columns = slice(first * width, last * width)
    return (
        jnp.dot(rows[:, :depth], weights[0][:, columns], preferred_element_type=F32)
        + jnp.dot(rows[:, depth:], weights[1][:, columns], preferred_element_type=F32)
    ).astype(BF)


def split(value, count):
    width = value.shape[1] // count
    return [value[:, k * width : (k + 1) * width] for k in range(count)]


def reduce_ring_first(rows, weights):
    up = tok_send(product(rows, weights, 0, 2), Z_UP)
    down = tok_send(product(rows, weights, 2, 4), Z_DOWN)
    near_up, near, far, far_down = split(product(rows, weights, 4, 8), 4)
    near_in, far_in = split(up, 2)
    far_more, near_more = split(down, 2)
    near_up = tok_send(add(near_up, near_in), Z_UP)
    far_down = tok_send(add(far_down, far_more), Z_DOWN)
    across = tok_send(add(far, far_in, far_down), X_SWAP)
    return [add(near, near_more), near_up, across]


def reduce_pair_first(rows, weights):
    far1, far2 = split(tok_send(product(rows, weights, 1, 3), X_SWAP), 2)
    far0, far3 = split(tok_send(product(rows, weights, 6, 8), X_SWAP), 2)
    near2 = product(rows, weights, 0, 1)
    near3, near1, near0 = split(product(rows, weights, 3, 6), 3)
    half = rows.shape[0] // 2
    first, second = slice(0, half), slice(half, None)

    def both(near, far, side):
        return near[side].astype(F32) + far[side].astype(F32)

    up = tok_send(jnp.stack([both(near2, far2, first), both(near1, far1, second)]).astype(BF), Z_UP)
    down = tok_send(jnp.stack([both(near2, far2, second), both(near3, far3, first)]).astype(BF), Z_DOWN)
    from_below = tok_send((both(near1, far1, first) + up[0].astype(F32)).astype(BF), Z_UP)
    from_above = tok_send((both(near3, far3, second) + down[0].astype(F32)).astype(BF), Z_DOWN)
    return [
        jnp.concatenate(
            [
                both(near0, far0, first) + down[1].astype(F32) + from_below.astype(F32),
                both(near0, far0, second) + up[1].astype(F32) + from_above.astype(F32),
            ]
        ).astype(BF)
    ]


def features(block):
    half = LANES // 2
    low = lax.broadcasted_iota(jnp.int32, (1, LANES), 1) < half
    first, second, third = (block[:, k * LANES : (k + 1) * LANES] for k in range(3))
    return (
        jnp.where(low, first, second),
        jnp.where(low, pltpu.roll(first, half, 1), pltpu.roll(third, half, 1)),
        jnp.where(low, second, third),
    )


def every(ref, row, length):
    return ref[pl.ds(row, BLOCKS, stride=length), :]


def local_kernel(groups, counts, where_ref, taps_ref, rates_ref, *refs):
    flat = sum(counts)
    starts = [sum(counts[:g]) for g in range(len(counts))]
    term_refs = [refs[start : start + count] for start, count in zip(starts, counts)]
    query_ref, gate_ref, edge_ref = refs[flat : flat + 3]
    raw_refs = refs[flat + 3 : flat + 6]
    key_ref, value_ref = refs[flat + 6 :]
    length = gate_ref.shape[0] // BLOCKS
    order = rates_ref.shape[0]
    rows = lax.broadcasted_iota(jnp.int32, (length, LANES), 0)
    for refs_here, group in zip(term_refs, groups):
        for place, (dy, dx) in enumerate(group):
            here = slice(place * length, (place + 1) * length)
            block = refs_here[0][here, :].astype(F32)
            for ref in refs_here[1:]:
                block = block + ref[here, :].astype(F32)
            spot = ((where_ref[3] + dy) & (Y - 1)) * XL + ((where_ref[4] + dx) & (XL - 1))
            there = pl.ds(pl.multiple_of(spot * length, length), length)
            mixed = []
            for f, raw in enumerate(features(block)):
                raw_refs[f][there, :] = raw
                total = taps_ref[f, 0:1, :] * raw
                for back in (1, 2):
                    moved = jnp.where(rows >= back, pltpu.roll(raw, back, 0), 0.0)
                    total = total + taps_ref[f, back : back + 1, :] * moved
                mixed.append(total)
            query_ref[there, :] = mixed[0]
            key_ref[there, :] = mixed[1]
            value_ref[there, :] = mixed[2]
            gate_ref[there, :] = mixed[1] * mixed[2]
    decay = [
        jnp.broadcast_to(jnp.exp(-rates_ref[n : n + 1, :]), (BLOCKS, LANES)) for n in range(order)
    ]

    def step(r, states):
        gate = every(gate_ref, r, length)
        return tuple(decay[n] * states[n] + gate for n in range(order))

    states = lax.fori_loop(
        2, length, step, tuple(jnp.zeros((BLOCKS, LANES), F32) for _ in range(order)), unroll=6
    )
    for n in range(order):
        edge_ref[n] = states[n]
    at = order
    for r in (0, 1):
        edge_ref[at] = every(key_ref, r, length)
        edge_ref[at + 1] = every(value_ref, r, length)
        at += 2
    for f in range(3):
        for r in (length - 1, length - 2):
            edge_ref[at] = every(raw_refs[f], r, length)
            at += 1


def filter_kernel(where_ref, taps_ref, rates_ref, weights_ref, skip_ref, mine_ref, theirs_ref, query_ref, gate_ref, out_ref, work):
    length = gate_ref.shape[0] // BLOCKS
    order = rates_ref.shape[0]
    core = where_ref[2]
    first = core == 0
    spots = lax.broadcasted_iota(jnp.int32, (BLOCKS, LANES), 0)

    def later(value, count):
        return jnp.where(spots >= count, pltpu.roll(value, count, 0), 0.0)

    def tap(f, back):
        return taps_ref[f, back : back + 1, :]

    def head(ref, before_ref, is_first):
        def before(f, back):
            value = before_ref[order + 4 + 2 * f + back - 1]
            return jnp.where(is_first, later(value, 1), value)

        key0 = ref[order] + tap(1, 1) * before(1, 1) + tap(1, 2) * before(1, 2)
        value0 = ref[order + 1] + tap(2, 1) * before(2, 1) + tap(2, 2) * before(2, 2)
        key1 = ref[order + 2] + tap(1, 2) * before(1, 1)
        value1 = ref[order + 3] + tap(2, 2) * before(2, 1)
        query0 = tap(0, 1) * before(0, 1) + tap(0, 2) * before(0, 2)
        query1 = tap(0, 2) * before(0, 1)
        return key0 * value0, key1 * value1, query0, query1

    gate0, gate1, query0, query1 = head(mine_ref, theirs_ref, first)
    their0, their1, _, _ = head(theirs_ref, mine_ref, jnp.logical_not(first))
    decay, states = [], []
    for n in range(order):
        rate = rates_ref[n : n + 1, :]
        factor0, factor1 = jnp.exp(-(length - 1) * rate), jnp.exp(-(length - 2) * rate)
        ours = mine_ref[n] + factor0 * gate0 + factor1 * gate1
        theirs = theirs_ref[n] + factor0 * their0 + factor1 * their1
        early, late = jnp.where(first, ours, theirs), jnp.where(first, theirs, ours)
        half = jnp.exp(-length * rate)
        total = half * early + late
        for count in (1, 2, 4):
            total = total + jnp.exp(-(2 * length * count) * rate) * later(total, count)
        before = later(total, 1)
        states.append(jnp.where(first, before, half * before + early))
        decay.append(jnp.broadcast_to(jnp.exp(-rate), (BLOCKS, LANES)))
    weights = [jnp.broadcast_to(weights_ref[n : n + 1, :], (BLOCKS, LANES)) for n in range(order)]
    skip = jnp.broadcast_to(skip_ref[...], (BLOCKS, LANES))

    def advance(r, states, gate, query):
        states = tuple(decay[n] * states[n] + gate for n in range(order))
        terms = [weights[n] * states[n] for n in range(order)] + [skip * gate]
        while len(terms) > 1:
            terms = [a + b for a, b in zip(terms[::2], terms[1::2])] + terms[len(terms) // 2 * 2 :]
        work[pl.ds(r, BLOCKS, stride=length), :] = query * terms[0]
        return states

    states = advance(0, tuple(states), gate0, every(query_ref, 0, length) + query0)
    states = advance(1, states, gate1, every(query_ref, 1, length) + query1)
    lax.fori_loop(
        2,
        length,
        lambda r, states: advance(r, states, every(gate_ref, r, length), every(query_ref, r, length)),
        states,
        unroll=6,
    )
    for g in range(XL):
        for dy in range(Y):
            spot = ((where_ref[3] + dy) & (Y - 1)) * XL + ((where_ref[4] + g) & (XL - 1))
            there = pl.ds(pl.multiple_of(spot * length, length), length)
            place = (g * Y + dy) * length
            out_ref[place : place + length, :] = work[there, :].astype(BF)


def own_lanes(shape):
    return pl.BlockSpec(shape, lambda _, where_ref: (0,) * (len(shape) - 1) + (where_ref[5],))


def local_part(where, taps, rates, groups, blocks):
    tokens = sum(len(group) for group in blocks) * blocks_length(groups[0][0], blocks[0])
    flat = [term for terms in groups for term in terms]
    edges = (rates.shape[0] + 10, BLOCKS, LANES)
    tall = jax.ShapeDtypeStruct((tokens, LANES), F32)
    return pl.pallas_call(
        lambda *refs: local_kernel(blocks, [len(terms) for terms in groups], *refs),
        out_shape=(tall, tall, jax.ShapeDtypeStruct(edges, F32)),
        grid_spec=pltpu.PrefetchScalarGridSpec(
            num_scalar_prefetch=1,
            grid=(1,),
            in_specs=[own_lanes(taps.shape[:-1] + (LANES,)), own_lanes(rates.shape[:-1] + (LANES,))]
            + [whole(term.shape) for term in flat],
            out_specs=[whole(tall.shape), whole(tall.shape), whole(edges)],
            scratch_shapes=[pltpu.VMEM((tokens, LANES), F32)] * 5,
        ),
        name="local_part",
    )(where, taps, rates, *flat)


def blocks_length(term, group):
    return term.shape[0] // len(group)


def filtered(where, taps, rates, weights, skip, mine, theirs, query, gate):
    return pl.pallas_call(
        filter_kernel,
        out_shape=jax.ShapeDtypeStruct(gate.shape, BF),
        grid_spec=pltpu.PrefetchScalarGridSpec(
            num_scalar_prefetch=1,
            grid=(1,),
            in_specs=[own_lanes(array.shape[:-1] + (LANES,)) for array in (taps, rates, weights, skip)]
            + [whole(array.shape) for array in (mine, theirs, query, gate)],
            out_specs=whole(gate.shape),
            scratch_shapes=[pltpu.VMEM(gate.shape, F32)],
        ),
        name="filtered",
    )(where, taps, rates, weights, skip, mine, theirs, query, gate)


def body(activations, proj_weight, short_taps, residues, decay_rates, skip_gain, out_weight):
    tok_index = lax.axis_index("tok")
    ch_index = lax.axis_index("ch")
    z, xh, core = tok_index >> 2, (tok_index >> 1) & 1, tok_index & 1
    y, xl = ch_index >> 1, ch_index & 1
    where = jnp.stack([z, xh, core, y, xl, ch_index * (Z * XH) + (tok_index >> 1)]).astype(jnp.int32)
    length = activations.shape[0] // CORES

    kept = lax.dynamic_slice_in_dim(activations, core * length, length, 0)
    other = swap(lax.dynamic_slice_in_dim(activations, (1 - core) * length, length, 0))
    mine = jnp.concatenate([kept, other], axis=1)
    mine, proj_weight = lax.optimization_barrier((mine, proj_weight))
    ordered = by_target(proj_weight, where, TARGETS, 1)
    weights = (ordered, swap(ordered))

    def along(value, dy):
        return ch_send(value, ch_perm(lambda y, xl: (y - dy, xl)))

    across = ch_send(mine, ch_perm(lambda y, xl: (y, 1 - xl)))
    blocks = [[(0, 0), (1, 0), (3, 0), (2, 0), (0, 1)], [(1, 1), (3, 1), (2, 1)]]
    first = [mine] + [along(mine, dy) for dy, _ in blocks[0][1:4]] + [across]
    first, weights = lax.optimization_barrier((first, weights))
    second = [along(first[-1], dy) for dy, _ in blocks[1]]
    second, out_weight = lax.optimization_barrier((second, out_weight))
    chips = [(k // XH, k % XH) for k in range(Z * XH)]
    out_ordered = by_target(out_weight, where, chips, 0)
    out_rows = jnp.concatenate([out_ordered, swap(out_ordered)], axis=1)
    groups = [
        reduce_ring_first(jnp.concatenate(first), weights),
        reduce_pair_first(jnp.concatenate(second), weights),
    ]
    groups, out_rows = lax.optimization_barrier((groups, out_rows))
    query, gate, edges = local_part(where, short_taps, decay_rates, groups, blocks)
    their_edges = swap(edges)
    gated = filtered(where, short_taps, decay_rates, residues, skip_gain[None], edges, their_edges, query, gate)

    pieces = [gated]
    for dz, dx in chips[1:]:
        pieces.append(tok_send(gated, tok_perm(lambda z, xh, c, dz=dz, dx=dx: (z - dz, xh ^ dx, c))))
    gathered = jnp.concatenate(pieces, axis=1)
    terms = []
    for k in range(BLOCKS):
        dx, dy = k // Y, k % Y
        rows = gathered[k * length : (k + 1) * length]
        term = jnp.dot(rows, out_rows, preferred_element_type=F32).astype(BF)
        if k:
            term = ch_send(term, ch_perm(lambda y, xl, dx=dx, dy=dy: (y + dy, xl ^ dx)))
        terms.append(term)
    total = add(*terms)
    cols = out_weight.shape[1]
    kept, other = total[:, :cols], swap(total[:, cols:])
    return jnp.where(core == 0, jnp.concatenate([kept, other]), jnp.concatenate([other, kept]))


def solution(mesh):
    return jax.shard_map(
        body,
        mesh=mesh,
        in_specs=(P("ch", "tok"), P("tok", "ch"), P(), P(), P(), P(), P("ch", "tok")),
        out_specs=P("ch", "tok"),
        check_vma=False,
    )
```

```python
import jax
import jax.numpy as jnp
from jax import lax
from jax.experimental import pallas as pl
from jax.experimental.pallas import tpu as pltpu
from jax.sharding import PartitionSpec as P

Z, XH, CORES = 4, 2, 2
Y, XL = 4, 2
BLOCKS = Y * XL
LANES = 128
BF = jnp.bfloat16
F32 = jnp.float32


def tok_perm(move):
    pairs = []
    for z in range(Z):
        for xh in range(XH):
            for c in range(CORES):
                nz, nx, nc = move(z, xh, c)
                pairs.append(((z * XH + xh) * CORES + c, ((nz % Z) * XH + nx) * CORES + nc))
    return pairs


def ch_perm(move):
    pairs = []
    for y in range(Y):
        for xl in range(XL):
            ny, nx = move(y, xl)
            pairs.append((y * XL + xl, (ny % Y) * XL + nx))
    return pairs


CORE_SWAP = tok_perm(lambda z, xh, c: (z, xh, 1 - c))
Z_UP = tok_perm(lambda z, xh, c: (z + 1, xh, c))
Z_DOWN = tok_perm(lambda z, xh, c: (z - 1, xh, c))
X_SWAP = tok_perm(lambda z, xh, c: (z, 1 - xh, c))


def tok_send(value, perm):
    return lax.ppermute(value, "tok", perm)


def ch_send(value, perm):
    return lax.ppermute(value, "ch", perm)


def swap(value):
    return tok_send(value, CORE_SWAP)


def add(*terms):
    total = terms[0].astype(F32)
    for term in terms[1:]:
        total = total + term.astype(F32)
    return total.astype(BF)


def whole(shape):
    return pl.BlockSpec(shape, lambda *_: (0,) * len(shape))


PLACES = [(2, 1), (1, 0), (1, 1), (3, 0), (3, 1), (2, 0), (0, 1), (0, 0)]
TARGETS = [(2, 0), (1, 1), (2, 1), (3, 0), (1, 0), (0, 0), (0, 1), (3, 1)]


def reorder_kernel(in_ref, *refs):
    out_refs, sems = refs[:-1], refs[-1]
    chip = lax.axis_index("tok") >> 1
    size = in_ref.shape[1] // len(TARGETS)
    each = len(TARGETS) // len(out_refs)
    copies = []
    for k, (dz, dx) in enumerate(TARGETS):
        target = (((chip >> 1) + dz) & (Z - 1)) * XH + ((chip + dx) & (XH - 1))
        source = pl.ds(pl.multiple_of(target * size, size), size)
        place = pl.ds(k % each * size, size)
        copies.append(
            pltpu.make_async_copy(in_ref.at[:, source], out_refs[k // each].at[:, place], sems.at[k])
        )
        copies[-1].start()
    for copy in copies:
        copy.wait()


def by_target(weight, parts):
    shape = jax.ShapeDtypeStruct((weight.shape[0], weight.shape[1] // parts), weight.dtype)
    return pl.pallas_call(
        reorder_kernel,
        out_shape=[shape] * parts,
        in_specs=[pl.BlockSpec(memory_space=pl.ANY)],
        out_specs=[pl.BlockSpec(memory_space=pltpu.VMEM)] * parts,
        scratch_shapes=[pltpu.SemaphoreType.DMA((len(TARGETS),))],
        name="by_target",
    )(weight)


def product(rows, weights, first, last):
    own, other = weights
    depth, cols = own[0].shape
    each = len(TARGETS) // len(own)
    width = cols // each
    outs = []
    for part in range(len(own)):
        low, high = max(first - part * each, 0), min(last - part * each, each)
        if low < high:
            columns = slice(low * width, high * width)
            outs.append(
                jnp.dot(rows[:, :depth], own[part][:, columns], preferred_element_type=F32)
                + jnp.dot(rows[:, depth:], other[part][:, columns], preferred_element_type=F32)
            )
    return jnp.concatenate(outs, axis=1).astype(BF)


def split(value, count):
    width = value.shape[1] // count
    return [value[:, k * width : (k + 1) * width] for k in range(count)]


def reduce_ring_first(rows, weights):
    up = tok_send(product(rows, weights, 0, 2), Z_UP)
    down = tok_send(product(rows, weights, 2, 4), Z_DOWN)
    near_up, near, far, far_down = split(product(rows, weights, 4, 8), 4)
    near_in, far_in = split(up, 2)
    far_more, near_more = split(down, 2)
    near_up = tok_send(add(near_up, near_in), Z_UP)
    far_down = tok_send(add(far_down, far_more), Z_DOWN)
    across = tok_send(add(far, far_in, far_down), X_SWAP)
    return [add(near, near_more), near_up, across]


def reduce_pair_first(rows, weights):
    far1, far2 = split(tok_send(product(rows, weights, 1, 3), X_SWAP), 2)
    far0, far3 = split(tok_send(product(rows, weights, 6, 8), X_SWAP), 2)
    near2 = product(rows, weights, 0, 1)
    near3 = product(rows, weights, 3, 4)
    near1, near0 = split(product(rows, weights, 4, 6), 2)
    half = rows.shape[0] // 2
    first, second = slice(0, half), slice(half, None)

    def both(near, far, side):
        return near[side].astype(F32) + far[side].astype(F32)

    up = tok_send(jnp.stack([both(near2, far2, first), both(near1, far1, second)]).astype(BF), Z_UP)
    down = tok_send(jnp.stack([both(near2, far2, second), both(near3, far3, first)]).astype(BF), Z_DOWN)
    from_below = tok_send((both(near1, far1, first) + up[0].astype(F32)).astype(BF), Z_UP)
    from_above = tok_send((both(near3, far3, second) + down[0].astype(F32)).astype(BF), Z_DOWN)
    return [
        jnp.concatenate(
            [
                both(near0, far0, first) + down[1].astype(F32) + from_below.astype(F32),
                both(near0, far0, second) + up[1].astype(F32) + from_above.astype(F32),
            ]
        ).astype(BF)
    ]


def features(block):
    half = LANES // 2
    low = lax.broadcasted_iota(jnp.int32, (1, LANES), 1) < half
    first, second, third = (block[:, k * LANES : (k + 1) * LANES] for k in range(3))
    return (
        jnp.where(low, first, second),
        jnp.where(low, pltpu.roll(first, half, 1), pltpu.roll(third, half, 1)),
        jnp.where(low, second, third),
    )


def every(ref, row, length):
    return ref[pl.ds(row, BLOCKS, stride=length), :]


def local_kernel(groups, counts, where_ref, taps_ref, rates_ref, *refs):
    flat = sum(counts)
    starts = [sum(counts[:g]) for g in range(len(counts))]
    term_refs = [refs[start : start + count] for start, count in zip(starts, counts)]
    query_ref, gate_ref, edge_ref = refs[flat : flat + 3]
    raw_refs = refs[flat + 3 : flat + 6]
    key_ref, value_ref = refs[flat + 6 :]
    length = gate_ref.shape[0] // BLOCKS
    order = rates_ref.shape[0]
    rows = lax.broadcasted_iota(jnp.int32, (length, LANES), 0)
    for refs_here, group in zip(term_refs, groups):
        for place, (dy, dx) in enumerate(group):
            here = slice(place * length, (place + 1) * length)
            block = refs_here[0][here, :].astype(F32)
            for ref in refs_here[1:]:
                block = block + ref[here, :].astype(F32)
            spot = ((where_ref[3] + dy) & (Y - 1)) * XL + ((where_ref[4] + dx) & (XL - 1))
            there = pl.ds(pl.multiple_of(spot * length, length), length)
            mixed = []
            for f, raw in enumerate(features(block)):
                raw_refs[f][there, :] = raw
                total = taps_ref[f, 0:1, :] * raw
                for back in (1, 2):
                    moved = jnp.where(rows >= back, pltpu.roll(raw, back, 0), 0.0)
                    total = total + taps_ref[f, back : back + 1, :] * moved
                mixed.append(total)
            query_ref[there, :] = mixed[0]
            key_ref[there, :] = mixed[1]
            value_ref[there, :] = mixed[2]
            gate_ref[there, :] = mixed[1] * mixed[2]
    decay = [
        jnp.broadcast_to(jnp.exp(-rates_ref[n : n + 1, :]), (BLOCKS, LANES)) for n in range(order)
    ]

    def step(r, states):
        gate = every(gate_ref, r, length)
        return tuple(decay[n] * states[n] + gate for n in range(order))

    states = lax.fori_loop(
        2, length, step, tuple(jnp.zeros((BLOCKS, LANES), F32) for _ in range(order)), unroll=6
    )
    for n in range(order):
        edge_ref[n] = states[n]
    at = order
    for r in (0, 1):
        edge_ref[at] = every(key_ref, r, length)
        edge_ref[at + 1] = every(value_ref, r, length)
        at += 2
    for f in range(3):
        for r in (length - 1, length - 2):
            edge_ref[at] = every(raw_refs[f], r, length)
            at += 1


def filter_kernel(where_ref, taps_ref, rates_ref, weights_ref, skip_ref, mine_ref, theirs_ref, query_ref, gate_ref, out_ref, work):
    length = gate_ref.shape[0] // BLOCKS
    order = rates_ref.shape[0]
    core = where_ref[2]
    first = core == 0
    spots = lax.broadcasted_iota(jnp.int32, (BLOCKS, LANES), 0)

    def later(value, count):
        return jnp.where(spots >= count, pltpu.roll(value, count, 0), 0.0)

    def tap(f, back):
        return taps_ref[f, back : back + 1, :]

    def head(ref, before_ref, is_first):
        def before(f, back):
            value = before_ref[order + 4 + 2 * f + back - 1]
            return jnp.where(is_first, later(value, 1), value)

        key0 = ref[order] + tap(1, 1) * before(1, 1) + tap(1, 2) * before(1, 2)
        value0 = ref[order + 1] + tap(2, 1) * before(2, 1) + tap(2, 2) * before(2, 2)
        key1 = ref[order + 2] + tap(1, 2) * before(1, 1)
        value1 = ref[order + 3] + tap(2, 2) * before(2, 1)
        query0 = tap(0, 1) * before(0, 1) + tap(0, 2) * before(0, 2)
        query1 = tap(0, 2) * before(0, 1)
        return key0 * value0, key1 * value1, query0, query1

    gate0, gate1, query0, query1 = head(mine_ref, theirs_ref, first)
    their0, their1, _, _ = head(theirs_ref, mine_ref, jnp.logical_not(first))
    decay, states = [], []
    for n in range(order):
        rate = rates_ref[n : n + 1, :]
        factor0, factor1 = jnp.exp(-(length - 1) * rate), jnp.exp(-(length - 2) * rate)
        ours = mine_ref[n] + factor0 * gate0 + factor1 * gate1
        theirs = theirs_ref[n] + factor0 * their0 + factor1 * their1
        early, late = jnp.where(first, ours, theirs), jnp.where(first, theirs, ours)
        half = jnp.exp(-length * rate)
        total = half * early + late
        for count in (1, 2, 4):
            total = total + jnp.exp(-(2 * length * count) * rate) * later(total, count)
        before = later(total, 1)
        states.append(jnp.where(first, before, half * before + early))
        decay.append(jnp.broadcast_to(jnp.exp(-rate), (BLOCKS, LANES)))
    weights = [jnp.broadcast_to(weights_ref[n : n + 1, :], (BLOCKS, LANES)) for n in range(order)]
    skip = jnp.broadcast_to(skip_ref[...], (BLOCKS, LANES))

    def advance(r, states, gate, query):
        states = tuple(decay[n] * states[n] + gate for n in range(order))
        terms = [weights[n] * states[n] for n in range(order)] + [skip * gate]
        while len(terms) > 1:
            terms = [a + b for a, b in zip(terms[::2], terms[1::2])] + terms[len(terms) // 2 * 2 :]
        work[pl.ds(r, BLOCKS, stride=length), :] = query * terms[0]
        return states

    states = advance(0, tuple(states), gate0, every(query_ref, 0, length) + query0)
    states = advance(1, states, gate1, every(query_ref, 1, length) + query1)
    lax.fori_loop(
        2,
        length,
        lambda r, states: advance(r, states, every(gate_ref, r, length), every(query_ref, r, length)),
        states,
        unroll=6,
    )
    for place, (dy, dx) in enumerate(PLACES):
        spot = ((where_ref[3] + dy) & (Y - 1)) * XL + ((where_ref[4] + dx) & (XL - 1))
        there = pl.ds(pl.multiple_of(spot * length, length), length)
        out_ref[place * length : (place + 1) * length, :] = work[there, :].astype(BF)


def own_lanes(shape):
    return pl.BlockSpec(shape, lambda _, where_ref: (0,) * (len(shape) - 1) + (where_ref[5],))


def local_part(where, taps, rates, groups, blocks):
    tokens = sum(len(group) for group in blocks) * blocks_length(groups[0][0], blocks[0])
    flat = [term for terms in groups for term in terms]
    edges = (rates.shape[0] + 10, BLOCKS, LANES)
    tall = jax.ShapeDtypeStruct((tokens, LANES), F32)
    return pl.pallas_call(
        lambda *refs: local_kernel(blocks, [len(terms) for terms in groups], *refs),
        out_shape=(tall, tall, jax.ShapeDtypeStruct(edges, F32)),
        grid_spec=pltpu.PrefetchScalarGridSpec(
            num_scalar_prefetch=1,
            grid=(1,),
            in_specs=[own_lanes(taps.shape[:-1] + (LANES,)), own_lanes(rates.shape[:-1] + (LANES,))]
            + [whole(term.shape) for term in flat],
            out_specs=[whole(tall.shape), whole(tall.shape), whole(edges)],
            scratch_shapes=[pltpu.VMEM((tokens, LANES), F32)] * 5,
        ),
        name="local_part",
    )(where, taps, rates, *flat)


def blocks_length(term, group):
    return term.shape[0] // len(group)


def filtered(where, taps, rates, weights, skip, mine, theirs, query, gate):
    return pl.pallas_call(
        filter_kernel,
        out_shape=jax.ShapeDtypeStruct(gate.shape, BF),
        grid_spec=pltpu.PrefetchScalarGridSpec(
            num_scalar_prefetch=1,
            grid=(1,),
            in_specs=[own_lanes(array.shape[:-1] + (LANES,)) for array in (taps, rates, weights, skip)]
            + [whole(array.shape) for array in (mine, theirs, query, gate)],
            out_specs=whole(gate.shape),
            scratch_shapes=[pltpu.VMEM(gate.shape, F32)],
        ),
        name="filtered",
    )(where, taps, rates, weights, skip, mine, theirs, query, gate)


def body(activations, proj_weight, short_taps, residues, decay_rates, skip_gain, out_weight):
    tok_index = lax.axis_index("tok")
    ch_index = lax.axis_index("ch")
    z, xh, core = tok_index >> 2, (tok_index >> 1) & 1, tok_index & 1
    y, xl = ch_index >> 1, ch_index & 1
    where = jnp.stack([z, xh, core, y, xl, ch_index * (Z * XH) + (tok_index >> 1)]).astype(jnp.int32)
    length = activations.shape[0] // CORES

    kept = lax.dynamic_slice_in_dim(activations, core * length, length, 0)
    other = swap(lax.dynamic_slice_in_dim(activations, (1 - core) * length, length, 0))
    mine = jnp.concatenate([kept, other], axis=1)
    mine, proj_weight = lax.optimization_barrier((mine, proj_weight))

    def along(value, dy):
        return ch_send(value, ch_perm(lambda y, xl: (y - dy, xl)))

    def across(value):
        return ch_send(value, ch_perm(lambda y, xl: (y, 1 - xl)))

    blocks = [[(0, 0), (1, 0), (3, 0), (2, 0), (0, 1)], [(1, 1), (3, 1), (2, 1)]]
    first = [mine, along(mine, 1), along(mine, 3), along(mine, 2), across(mine)]
    ordered = by_target(proj_weight, 2)
    early, late = swap(ordered[0]), swap(ordered[1])
    first, early = lax.optimization_barrier((first, early))
    second = [along(first[4], 1), along(first[4], 3), across(first[3])]
    weights = (ordered, [early, late])
    groups = [
        reduce_ring_first(jnp.concatenate(first), weights),
        reduce_pair_first(jnp.concatenate(second), weights),
    ]
    query, gate, edges = local_part(where, short_taps, decay_rates, groups, blocks)
    edges, out_weight = lax.optimization_barrier((edges, out_weight))
    their_edges = swap(edges)
    their_out = swap(out_weight)
    gated = filtered(where, short_taps, decay_rates, residues, skip_gain[None], edges, their_edges, query, gate)

    gated, their_out = lax.optimization_barrier((gated, their_out))
    out_rows = jnp.concatenate([out_weight, their_out], axis=1)

    pieces = {(0, 0): gated}
    pieces[0, 1] = tok_send(gated, X_SWAP)
    pieces[2, 0] = tok_send(gated, tok_perm(lambda z, xh, c: (z + 2, xh, c)))
    pieces[1, 0], pieces[3, 0] = tok_send(gated, Z_DOWN), tok_send(gated, Z_UP)
    pieces[1, 1], pieces[3, 1] = tok_send(pieces[0, 1], Z_DOWN), tok_send(pieces[0, 1], Z_UP)
    pieces[2, 1] = tok_send(pieces[2, 0], X_SWAP)
    gathered = jnp.zeros((gated.shape[0], Z * XH * LANES), BF)
    for (dz, dx), piece in pieces.items():
        chip = ((z + dz) & (Z - 1)) * XH + ((xh + dx) & (XH - 1))
        gathered = lax.dynamic_update_slice(gathered, piece, (0, chip * LANES))

    def part(first, last):
        rows = gathered[PLACES.index(first) * length : (PLACES.index(last) + 1) * length]
        return jnp.dot(rows, out_rows, preferred_element_type=F32)

    def forward(value, dy):
        return ch_send(value, ch_perm(lambda y, xl: (y + dy, xl)))

    far = across(part((2, 1), (2, 1)).astype(BF))
    up = forward(part((1, 0), (1, 1)).astype(BF), 1)
    down = forward(part((3, 0), (3, 1)).astype(BF), 3)
    opposite = forward((part((2, 0), (2, 0)) + far.astype(F32)).astype(BF), 2)
    beside = across(
        (part((0, 1), (0, 1)) + up[length:].astype(F32) + down[length:].astype(F32)).astype(BF)
    )
    total = part((0, 0), (0, 0))
    for term in (up[:length], down[:length], opposite, beside):
        total = total + term.astype(F32)
    total = total.astype(BF)
    cols = out_weight.shape[1]
    kept, other = total[:, :cols], swap(total[:, cols:])
    return jnp.where(core == 0, jnp.concatenate([kept, other]), jnp.concatenate([other, kept]))


def solution(mesh):
    return jax.shard_map(
        body,
        mesh=mesh,
        in_specs=(P("ch", "tok"), P("tok", "ch"), P(), P(), P(), P(), P("ch", "tok")),
        out_specs=P("ch", "tok"),
        check_vma=False,
    )
```

```python
import jax
import jax.numpy as jnp
from jax import lax
from jax.experimental import pallas as pl
from jax.experimental.pallas import tpu as pltpu
from jax.sharding import PartitionSpec as P

Z, XH, CORES = 4, 2, 2
Y, XL = 4, 2
BLOCKS = Y * XL
LANES = 128
BF = jnp.bfloat16
F32 = jnp.float32


def tok_perm(move):
    pairs = []
    for z in range(Z):
        for xh in range(XH):
            for c in range(CORES):
                nz, nx, nc = move(z, xh, c)
                pairs.append(((z * XH + xh) * CORES + c, ((nz % Z) * XH + nx) * CORES + nc))
    return pairs


def ch_perm(move):
    pairs = []
    for y in range(Y):
        for xl in range(XL):
            ny, nx = move(y, xl)
            pairs.append((y * XL + xl, (ny % Y) * XL + nx))
    return pairs


CORE_SWAP = tok_perm(lambda z, xh, c: (z, xh, 1 - c))
Z_UP = tok_perm(lambda z, xh, c: (z + 1, xh, c))
Z_DOWN = tok_perm(lambda z, xh, c: (z - 1, xh, c))
X_SWAP = tok_perm(lambda z, xh, c: (z, 1 - xh, c))


def tok_send(value, perm):
    return lax.ppermute(value, "tok", perm)


def ch_send(value, perm):
    return lax.ppermute(value, "ch", perm)


def swap(value):
    return tok_send(value, CORE_SWAP)


def add(*terms):
    total = terms[0].astype(F32)
    for term in terms[1:]:
        total = total + term.astype(F32)
    return total.astype(BF)


def whole(shape):
    return pl.BlockSpec(shape, lambda *_: (0,) * len(shape))


PLACES = [(2, 1), (1, 0), (1, 1), (3, 0), (3, 1), (2, 0), (0, 1), (0, 0)]
TARGETS = [(2, 0), (1, 1), (2, 1), (3, 0), (1, 0), (0, 0), (0, 1), (3, 1)]


def reorder_kernel(parts, in_ref, *refs):
    out_refs, sems = refs[:-1], refs[-1]
    chip = lax.axis_index("tok") >> 1
    size = in_ref.shape[1] // len(TARGETS)
    copies = []
    for targets, out_ref in zip(parts, out_refs):
        for k, (dz, dx) in enumerate(targets):
            target = (((chip >> 1) + dz) & (Z - 1)) * XH + ((chip + dx) & (XH - 1))
            source = pl.ds(pl.multiple_of(target * size, size), size)
            place = pl.ds(k * size, size)
            sem = sems.at[len(copies)]
            copies.append(pltpu.make_async_copy(in_ref.at[:, source], out_ref.at[:, place], sem))
            copies[-1].start()
    for copy in copies:
        copy.wait()


def by_target(weight, *parts):
    width = weight.shape[1] // len(TARGETS)
    return pl.pallas_call(
        lambda *refs: reorder_kernel(parts, *refs),
        out_shape=[
            jax.ShapeDtypeStruct((weight.shape[0], width * len(targets)), weight.dtype) for targets in parts
        ],
        in_specs=[pl.BlockSpec(memory_space=pl.ANY)],
        out_specs=[pl.BlockSpec(memory_space=pltpu.VMEM)] * len(parts),
        scratch_shapes=[pltpu.SemaphoreType.DMA((sum(len(targets) for targets in parts),))],
        name="by_target",
    )(weight)


def product(rows, weights, first, last):
    own, other = weights
    depth, cols = own[0].shape
    each = len(TARGETS) // 2
    width = cols // each
    outs = []
    for part in range(len(own)):
        low, high = max(first - part * each, 0), min(last - part * each, each)
        if low < high:
            columns = slice(low * width, high * width)
            outs.append(
                jnp.dot(rows[:, :depth], own[part][:, columns], preferred_element_type=F32)
                + jnp.dot(rows[:, depth:], other[part][:, columns], preferred_element_type=F32)
            )
    return jnp.concatenate(outs, axis=1).astype(BF)


def split(value, count):
    width = value.shape[1] // count
    return [value[:, k * width : (k + 1) * width] for k in range(count)]


def reduce_groups(rows, leaving, late_rows, weights):
    up, down = tok_send(leaving[0], Z_UP), tok_send(leaving[1], Z_DOWN)
    rows, late_rows = lax.optimization_barrier((rows, late_rows))
    near_up, near, far, far_down = split(product(rows, weights, 4, 8), 4)

    far1, far2 = split(tok_send(product(late_rows, weights, 1, 3), X_SWAP), 2)
    far0, far3 = split(tok_send(product(late_rows, weights, 6, 8), X_SWAP), 2)
    near2 = product(late_rows, weights, 0, 1)
    near3 = product(late_rows, weights, 3, 4)
    near1, near0 = split(product(late_rows, weights, 4, 6), 2)
    near_in, far_in = split(up, 2)
    far_more, near_more = split(down, 2)
    far_down = tok_send(add(far_down, far_more), Z_DOWN)
    near_up = tok_send(add(near_up, near_in), Z_UP)
    near_up, far_down, near0, near1, near2, near3 = lax.optimization_barrier(
        (near_up, far_down, near0, near1, near2, near3)
    )
    crossed = tok_send(add(far, far_in, far_down), X_SWAP)
    terms = [add(near, near_more), near_up, crossed]

    half = late_rows.shape[0] // 2
    first, second = slice(0, half), slice(half, None)

    def both(near, far, side):
        return near[side].astype(F32) + far[side].astype(F32)

    up = tok_send(jnp.stack([both(near2, far2, first), both(near1, far1, second)]).astype(BF), Z_UP)
    down = tok_send(jnp.stack([both(near2, far2, second), both(near3, far3, first)]).astype(BF), Z_DOWN)
    from_below = tok_send((both(near1, far1, first) + up[0].astype(F32)).astype(BF), Z_UP)
    from_above = tok_send((both(near3, far3, second) + down[0].astype(F32)).astype(BF), Z_DOWN)
    late_terms = [
        jnp.concatenate(
            [
                both(near0, far0, first) + down[1].astype(F32) + from_below.astype(F32),
                both(near0, far0, second) + up[1].astype(F32) + from_above.astype(F32),
            ]
        ).astype(BF)
    ]
    return [terms, late_terms]


def features(block):
    half = LANES // 2
    low = lax.broadcasted_iota(jnp.int32, (1, LANES), 1) < half
    first, second, third = (block[:, k * LANES : (k + 1) * LANES] for k in range(3))
    return (
        jnp.where(low, first, second),
        jnp.where(low, pltpu.roll(first, half, 1), pltpu.roll(third, half, 1)),
        jnp.where(low, second, third),
    )


def every(ref, row, length):
    return ref[pl.ds(row, BLOCKS, stride=length), :]


def local_kernel(groups, counts, where_ref, taps_ref, rates_ref, *refs):
    flat = sum(counts)
    starts = [sum(counts[:g]) for g in range(len(counts))]
    term_refs = [refs[start : start + count] for start, count in zip(starts, counts)]
    query_ref, gate_ref, edge_ref = refs[flat : flat + 3]
    raw_refs = refs[flat + 3 : flat + 6]
    key_ref, value_ref = refs[flat + 6 :]
    length = gate_ref.shape[0] // BLOCKS
    order = rates_ref.shape[0]
    rows = lax.broadcasted_iota(jnp.int32, (length, LANES), 0)
    for refs_here, group in zip(term_refs, groups):
        for place, (dy, dx) in enumerate(group):
            here = slice(place * length, (place + 1) * length)
            block = refs_here[0][here, :].astype(F32)
            for ref in refs_here[1:]:
                block = block + ref[here, :].astype(F32)
            spot = ((where_ref[3] + dy) & (Y - 1)) * XL + ((where_ref[4] + dx) & (XL - 1))
            there = pl.ds(pl.multiple_of(spot * length, length), length)
            mixed = []
            for f, raw in enumerate(features(block)):
                raw_refs[f][there, :] = raw
                total = taps_ref[f, 0:1, :] * raw
                for back in (1, 2):
                    moved = jnp.where(rows >= back, pltpu.roll(raw, back, 0), 0.0)
                    total = total + taps_ref[f, back : back + 1, :] * moved
                mixed.append(total)
            query_ref[there, :] = mixed[0]
            key_ref[there, :] = mixed[1]
            value_ref[there, :] = mixed[2]
            gate_ref[there, :] = mixed[1] * mixed[2]
    decay = [
        jnp.broadcast_to(jnp.exp(-rates_ref[n : n + 1, :]), (BLOCKS, LANES)) for n in range(order)
    ]

    def step(r, states):
        gate = every(gate_ref, r, length)
        return tuple(decay[n] * states[n] + gate for n in range(order))

    states = lax.fori_loop(
        2, length, step, tuple(jnp.zeros((BLOCKS, LANES), F32) for _ in range(order)), unroll=6
    )
    for n in range(order):
        edge_ref[n] = states[n]
    at = order
    for r in (0, 1):
        edge_ref[at] = every(key_ref, r, length)
        edge_ref[at + 1] = every(value_ref, r, length)
        at += 2
    for f in range(3):
        for r in (length - 1, length - 2):
            edge_ref[at] = every(raw_refs[f], r, length)
            at += 1


def filter_kernel(where_ref, taps_ref, rates_ref, weights_ref, skip_ref, mine_ref, theirs_ref, query_ref, gate_ref, out_ref, work):
    length = gate_ref.shape[0] // BLOCKS
    order = rates_ref.shape[0]
    core = where_ref[2]
    first = core == 0
    spots = lax.broadcasted_iota(jnp.int32, (BLOCKS, LANES), 0)

    def later(value, count):
        return jnp.where(spots >= count, pltpu.roll(value, count, 0), 0.0)

    def tap(f, back):
        return taps_ref[f, back : back + 1, :]

    def head(ref, before_ref, is_first):
        def before(f, back):
            value = before_ref[order + 4 + 2 * f + back - 1]
            return jnp.where(is_first, later(value, 1), value)

        key0 = ref[order] + tap(1, 1) * before(1, 1) + tap(1, 2) * before(1, 2)
        value0 = ref[order + 1] + tap(2, 1) * before(2, 1) + tap(2, 2) * before(2, 2)
        key1 = ref[order + 2] + tap(1, 2) * before(1, 1)
        value1 = ref[order + 3] + tap(2, 2) * before(2, 1)
        query0 = tap(0, 1) * before(0, 1) + tap(0, 2) * before(0, 2)
        query1 = tap(0, 2) * before(0, 1)
        return key0 * value0, key1 * value1, query0, query1

    gate0, gate1, query0, query1 = head(mine_ref, theirs_ref, first)
    their0, their1, _, _ = head(theirs_ref, mine_ref, jnp.logical_not(first))
    decay, states = [], []
    for n in range(order):
        rate = rates_ref[n : n + 1, :]
        factor0, factor1 = jnp.exp(-(length - 1) * rate), jnp.exp(-(length - 2) * rate)
        ours = mine_ref[n] + factor0 * gate0 + factor1 * gate1
        theirs = theirs_ref[n] + factor0 * their0 + factor1 * their1
        early, late = jnp.where(first, ours, theirs), jnp.where(first, theirs, ours)
        half = jnp.exp(-length * rate)
        total = half * early + late
        for count in (1, 2, 4):
            total = total + jnp.exp(-(2 * length * count) * rate) * later(total, count)
        before = later(total, 1)
        states.append(jnp.where(first, before, half * before + early))
        decay.append(jnp.broadcast_to(jnp.exp(-rate), (BLOCKS, LANES)))
    weights = [jnp.broadcast_to(weights_ref[n : n + 1, :], (BLOCKS, LANES)) for n in range(order)]
    skip = jnp.broadcast_to(skip_ref[...], (BLOCKS, LANES))

    def advance(r, states, gate, query):
        states = tuple(decay[n] * states[n] + gate for n in range(order))
        terms = [weights[n] * states[n] for n in range(order)] + [skip * gate]
        while len(terms) > 1:
            terms = [a + b for a, b in zip(terms[::2], terms[1::2])] + terms[len(terms) // 2 * 2 :]
        work[pl.ds(r, BLOCKS, stride=length), :] = query * terms[0]
        return states

    states = advance(0, tuple(states), gate0, every(query_ref, 0, length) + query0)
    states = advance(1, states, gate1, every(query_ref, 1, length) + query1)
    lax.fori_loop(
        2,
        length,
        lambda r, states: advance(r, states, every(gate_ref, r, length), every(query_ref, r, length)),
        states,
        unroll=6,
    )
    for place, (dy, dx) in enumerate(PLACES):
        spot = ((where_ref[3] + dy) & (Y - 1)) * XL + ((where_ref[4] + dx) & (XL - 1))
        there = pl.ds(pl.multiple_of(spot * length, length), length)
        out_ref[place * length : (place + 1) * length, :] = work[there, :].astype(BF)


def own_lanes(shape):
    return pl.BlockSpec(shape, lambda _, where_ref: (0,) * (len(shape) - 1) + (where_ref[5],))


def local_part(where, taps, rates, groups, blocks):
    tokens = sum(len(group) for group in blocks) * blocks_length(groups[0][0], blocks[0])
    flat = [term for terms in groups for term in terms]
    edges = (rates.shape[0] + 10, BLOCKS, LANES)
    tall = jax.ShapeDtypeStruct((tokens, LANES), F32)
    return pl.pallas_call(
        lambda *refs: local_kernel(blocks, [len(terms) for terms in groups], *refs),
        out_shape=(tall, tall, jax.ShapeDtypeStruct(edges, F32)),
        grid_spec=pltpu.PrefetchScalarGridSpec(
            num_scalar_prefetch=1,
            grid=(1,),
            in_specs=[own_lanes(taps.shape[:-1] + (LANES,)), own_lanes(rates.shape[:-1] + (LANES,))]
            + [whole(term.shape) for term in flat],
            out_specs=[whole(tall.shape), whole(tall.shape), whole(edges)],
            scratch_shapes=[pltpu.VMEM((tokens, LANES), F32)] * 5,
        ),
        name="local_part",
    )(where, taps, rates, *flat)


def blocks_length(term, group):
    return term.shape[0] // len(group)


def filtered(where, taps, rates, weights, skip, mine, theirs, query, gate):
    return pl.pallas_call(
        filter_kernel,
        out_shape=jax.ShapeDtypeStruct(gate.shape, BF),
        grid_spec=pltpu.PrefetchScalarGridSpec(
            num_scalar_prefetch=1,
            grid=(1,),
            in_specs=[own_lanes(array.shape[:-1] + (LANES,)) for array in (taps, rates, weights, skip)]
            + [whole(array.shape) for array in (mine, theirs, query, gate)],
            out_specs=whole(gate.shape),
            scratch_shapes=[pltpu.VMEM(gate.shape, F32)],
        ),
        name="filtered",
    )(where, taps, rates, weights, skip, mine, theirs, query, gate)


def body(activations, proj_weight, short_taps, residues, decay_rates, skip_gain, out_weight):
    tok_index = lax.axis_index("tok")
    ch_index = lax.axis_index("ch")
    z, xh, core = tok_index >> 2, (tok_index >> 1) & 1, tok_index & 1
    y, xl = ch_index >> 1, ch_index & 1
    where = jnp.stack([z, xh, core, y, xl, ch_index * (Z * XH) + (tok_index >> 1)]).astype(jnp.int32)
    length = activations.shape[0] // CORES

    kept = lax.dynamic_slice_in_dim(activations, core * length, length, 0)
    other = lax.dynamic_slice_in_dim(activations, (1 - core) * length, length, 0)
    other, proj_weight = lax.optimization_barrier((other, proj_weight))
    other = swap(other)
    mine = jnp.concatenate([kept, other], axis=1)

    def along(value, dy):
        return ch_send(value, ch_perm(lambda y, xl: (y - dy, xl)))

    def across(value):
        return ch_send(value, ch_perm(lambda y, xl: (y, 1 - xl)))

    blocks = [[(0, 0), (1, 0), (3, 0), (2, 0), (0, 1)], [(1, 1), (3, 1), (2, 1)]]
    first = [mine, along(mine, 1), along(mine, 3), along(mine, 2), across(mine)]
    half = len(TARGETS) // 2
    early, late = by_target(proj_weight, TARGETS[:half], TARGETS[half:])
    early, late = (early, swap(early)), (late, swap(late))
    first[4], first[1], first[2], early = lax.optimization_barrier((first[4], first[1], first[2], early))
    second = [along(first[4], 1), along(first[4], 3), across(first[3])]
    weights = list(zip(early, late))
    rows = jnp.concatenate(first)
    leaving = product(rows, weights, 0, 2), product(rows, weights, 2, 4)
    groups = reduce_groups(rows, leaving, jnp.concatenate(second), weights)
    groups, out_weight = lax.optimization_barrier((groups, out_weight))
    query, gate, edges = local_part(where, short_taps, decay_rates, groups, blocks)
    edges, out_weight = lax.optimization_barrier((edges, out_weight))
    their_edges = swap(edges)
    their_out = swap(out_weight)
    gated = filtered(where, short_taps, decay_rates, residues, skip_gain[None], edges, their_edges, query, gate)

    gated, their_out = lax.optimization_barrier((gated, their_out))
    out_rows = jnp.concatenate([out_weight, their_out], axis=1)

    pieces = {(0, 0): gated}
    pieces[0, 1] = tok_send(gated, X_SWAP)
    pieces[2, 0] = tok_send(gated, tok_perm(lambda z, xh, c: (z + 2, xh, c)))
    pieces[1, 0], pieces[3, 0] = tok_send(gated, Z_DOWN), tok_send(gated, Z_UP)
    pieces[1, 1], pieces[3, 1] = tok_send(pieces[0, 1], Z_DOWN), tok_send(pieces[0, 1], Z_UP)
    pieces[2, 1] = tok_send(pieces[2, 0], X_SWAP)
    gathered = jnp.zeros((gated.shape[0], Z * XH * LANES), BF)
    for (dz, dx), piece in pieces.items():
        chip = ((z + dz) & (Z - 1)) * XH + ((xh + dx) & (XH - 1))
        gathered = lax.dynamic_update_slice(gathered, piece, (0, chip * LANES))

    def part(first, last):
        rows = gathered[PLACES.index(first) * length : (PLACES.index(last) + 1) * length]
        return jnp.dot(rows, out_rows, preferred_element_type=F32)

    def forward(value, dy):
        return ch_send(value, ch_perm(lambda y, xl: (y + dy, xl)))

    far = across(part((2, 1), (2, 1)).astype(BF))
    up, down = [forward(part((dy, 1), (dy, 1)).astype(BF), dy) for dy in (1, 3)]
    near_up, near_down = [forward(part((dy, 0), (dy, 0)).astype(BF), dy) for dy in (1, 3)]
    opposite = forward((part((2, 0), (2, 0)) + far.astype(F32)).astype(BF), 2)
    beside = across((part((0, 1), (0, 1)) + up.astype(F32) + down.astype(F32)).astype(BF))
    total = part((0, 0), (0, 0))
    for term in (near_up, near_down, opposite, beside):
        total = total + term.astype(F32)
    total = total.astype(BF)
    cols = out_weight.shape[1]
    kept, other = total[:, :cols], swap(total[:, cols:])
    return jnp.where(core == 0, jnp.concatenate([kept, other]), jnp.concatenate([other, kept]))


def solution(mesh):
    return jax.shard_map(
        body,
        mesh=mesh,
        in_specs=(P("ch", "tok"), P("tok", "ch"), P(), P(), P(), P(), P("ch", "tok")),
        out_specs=P("ch", "tok"),
        check_vma=False,
    )
```

```python
import jax
import jax.numpy as jnp
from jax import lax
from jax.experimental import pallas as pl
from jax.experimental.pallas import tpu as pltpu
from jax.sharding import PartitionSpec as P

Z, XH, CORES = 4, 2, 2
Y, XL = 4, 2
BLOCKS = Y * XL
LANES = 128
BF = jnp.bfloat16
F32 = jnp.float32


def tok_perm(move):
    pairs = []
    for z in range(Z):
        for xh in range(XH):
            for c in range(CORES):
                nz, nx, nc = move(z, xh, c)
                pairs.append(((z * XH + xh) * CORES + c, ((nz % Z) * XH + nx) * CORES + nc))
    return pairs


def ch_perm(move):
    pairs = []
    for y in range(Y):
        for xl in range(XL):
            ny, nx = move(y, xl)
            pairs.append((y * XL + xl, (ny % Y) * XL + nx))
    return pairs


CORE_SWAP = tok_perm(lambda z, xh, c: (z, xh, 1 - c))
Z_UP = tok_perm(lambda z, xh, c: (z + 1, xh, c))
Z_DOWN = tok_perm(lambda z, xh, c: (z - 1, xh, c))
X_SWAP = tok_perm(lambda z, xh, c: (z, 1 - xh, c))


def tok_send(value, perm):
    return lax.ppermute(value, "tok", perm)


def ch_send(value, perm):
    return lax.ppermute(value, "ch", perm)


def swap(value):
    return tok_send(value, CORE_SWAP)


def add(*terms):
    total = terms[0].astype(F32)
    for term in terms[1:]:
        total = total + term.astype(F32)
    return total.astype(BF)


def whole(shape):
    return pl.BlockSpec(shape, lambda *_: (0,) * len(shape))


PLACES = [(2, 1), (1, 0), (1, 1), (3, 0), (3, 1), (2, 0), (0, 1), (0, 0)]
TARGETS = [(2, 0), (1, 1), (2, 1), (3, 0), (1, 0), (0, 0), (0, 1), (3, 1)]


def reorder_kernel(parts, in_ref, *refs):
    out_refs, sems = refs[:-1], refs[-1]
    chip = lax.axis_index("tok") >> 1
    size = in_ref.shape[1] // len(TARGETS)
    copies = []
    for targets, out_ref in zip(parts, out_refs):
        for k, (dz, dx) in enumerate(targets):
            target = (((chip >> 1) + dz) & (Z - 1)) * XH + ((chip + dx) & (XH - 1))
            source = pl.ds(pl.multiple_of(target * size, size), size)
            place = pl.ds(k * size, size)
            sem = sems.at[len(copies)]
            copies.append(pltpu.make_async_copy(in_ref.at[:, source], out_ref.at[:, place], sem))
            copies[-1].start()
    for copy in copies:
        copy.wait()


def by_target(weight, *parts):
    width = weight.shape[1] // len(TARGETS)
    return pl.pallas_call(
        lambda *refs: reorder_kernel(parts, *refs),
        out_shape=[
            jax.ShapeDtypeStruct((weight.shape[0], width * len(targets)), weight.dtype) for targets in parts
        ],
        in_specs=[pl.BlockSpec(memory_space=pl.ANY)],
        out_specs=[pl.BlockSpec(memory_space=pltpu.VMEM)] * len(parts),
        scratch_shapes=[pltpu.SemaphoreType.DMA((sum(len(targets) for targets in parts),))],
        name="by_target",
    )(weight)


def product(rows, weights, first, last):
    own, other = weights
    depth, cols = own[0].shape
    each = len(TARGETS) // 2
    width = cols // each
    outs = []
    for part in range(len(own)):
        low, high = max(first - part * each, 0), min(last - part * each, each)
        if low < high:
            columns = slice(low * width, high * width)
            outs.append(
                jnp.dot(rows[:, :depth], own[part][:, columns], preferred_element_type=F32)
                + jnp.dot(rows[:, depth:], other[part][:, columns], preferred_element_type=F32)
            )
    return jnp.concatenate(outs, axis=1).astype(BF)


def split(value, count):
    width = value.shape[1] // count
    return [value[:, k * width : (k + 1) * width] for k in range(count)]


def reduce_groups(rows, leaving, late_rows, weights):
    up, down = tok_send(leaving[0], Z_UP), tok_send(leaving[1], Z_DOWN)
    rows, late_rows = lax.optimization_barrier((rows, late_rows))
    near_up, near, far, far_down = split(product(rows, weights, 4, 8), 4)

    far1, far2 = split(tok_send(product(late_rows, weights, 1, 3), X_SWAP), 2)
    far0, far3 = split(tok_send(product(late_rows, weights, 6, 8), X_SWAP), 2)
    near2 = product(late_rows, weights, 0, 1)
    near3 = product(late_rows, weights, 3, 4)
    near1, near0 = split(product(late_rows, weights, 4, 6), 2)
    near_in, far_in = split(up, 2)
    far_more, near_more = split(down, 2)
    far_down = tok_send(add(far_down, far_more), Z_DOWN)
    near_up = tok_send(add(near_up, near_in), Z_UP)
    near_up, far_down, near0, near1, near2, near3 = lax.optimization_barrier(
        (near_up, far_down, near0, near1, near2, near3)
    )
    crossed = tok_send(add(far, far_in, far_down), X_SWAP)
    terms = [add(near, near_more), near_up, crossed]

    half = late_rows.shape[0] // 2
    first, second = slice(0, half), slice(half, None)

    def both(near, far, side):
        return near[side].astype(F32) + far[side].astype(F32)

    up = tok_send(jnp.stack([both(near2, far2, first), both(near1, far1, second)]).astype(BF), Z_UP)
    down = tok_send(jnp.stack([both(near2, far2, second), both(near3, far3, first)]).astype(BF), Z_DOWN)
    from_below = tok_send((both(near1, far1, first) + up[0].astype(F32)).astype(BF), Z_UP)
    from_above = tok_send((both(near3, far3, second) + down[0].astype(F32)).astype(BF), Z_DOWN)
    late_terms = [
        jnp.concatenate(
            [
                both(near0, far0, first) + down[1].astype(F32) + from_below.astype(F32),
                both(near0, far0, second) + up[1].astype(F32) + from_above.astype(F32),
            ]
        ).astype(BF)
    ]
    return [terms, late_terms]


def features(block):
    half = LANES // 2
    low = lax.broadcasted_iota(jnp.int32, (1, LANES), 1) < half
    first, second, third = (block[:, k * LANES : (k + 1) * LANES] for k in range(3))
    return (
        jnp.where(low, first, second),
        jnp.where(low, pltpu.roll(first, half, 1), pltpu.roll(third, half, 1)),
        jnp.where(low, second, third),
    )


def every(ref, row, length):
    return ref[pl.ds(row, BLOCKS, stride=length), :]


def local_kernel(groups, counts, where_ref, taps_ref, rates_ref, *refs):
    flat = sum(counts)
    starts = [sum(counts[:g]) for g in range(len(counts))]
    term_refs = [refs[start : start + count] for start, count in zip(starts, counts)]
    query_ref, gate_ref, edge_ref = refs[flat : flat + 3]
    raw_refs = refs[flat + 3 : flat + 6]
    key_ref, value_ref = refs[flat + 6 :]
    length = gate_ref.shape[0] // BLOCKS
    order = rates_ref.shape[0]
    rows = lax.broadcasted_iota(jnp.int32, (length, LANES), 0)
    for refs_here, group in zip(term_refs, groups):
        for place, (dy, dx) in enumerate(group):
            here = slice(place * length, (place + 1) * length)
            block = refs_here[0][here, :].astype(F32)
            for ref in refs_here[1:]:
                block = block + ref[here, :].astype(F32)
            spot = ((where_ref[3] + dy) & (Y - 1)) * XL + ((where_ref[4] + dx) & (XL - 1))
            there = pl.ds(pl.multiple_of(spot * length, length), length)
            mixed = []
            for f, raw in enumerate(features(block)):
                raw_refs[f][there, :] = raw
                total = taps_ref[f, 0:1, :] * raw
                for back in (1, 2):
                    moved = jnp.where(rows >= back, pltpu.roll(raw, back, 0), 0.0)
                    total = total + taps_ref[f, back : back + 1, :] * moved
                mixed.append(total)
            query_ref[there, :] = mixed[0]
            key_ref[there, :] = mixed[1]
            value_ref[there, :] = mixed[2]
            gate_ref[there, :] = mixed[1] * mixed[2]
    decay = [
        jnp.broadcast_to(jnp.exp(-rates_ref[n : n + 1, :]), (BLOCKS, LANES)) for n in range(order)
    ]

    def step(r, states):
        gate = every(gate_ref, r, length)
        return tuple(decay[n] * states[n] + gate for n in range(order))

    states = lax.fori_loop(
        2, length, step, tuple(jnp.zeros((BLOCKS, LANES), F32) for _ in range(order)), unroll=6
    )
    for n in range(order):
        edge_ref[n] = states[n]
    at = order
    for r in (0, 1):
        edge_ref[at] = every(key_ref, r, length)
        edge_ref[at + 1] = every(value_ref, r, length)
        at += 2
    for f in range(3):
        for r in (length - 1, length - 2):
            edge_ref[at] = every(raw_refs[f], r, length)
            at += 1


def filter_kernel(where_ref, taps_ref, rates_ref, weights_ref, skip_ref, mine_ref, theirs_ref, query_ref, gate_ref, out_ref, work):
    length = gate_ref.shape[0] // BLOCKS
    order = rates_ref.shape[0]
    core = where_ref[2]
    first = core == 0
    spots = lax.broadcasted_iota(jnp.int32, (BLOCKS, LANES), 0)

    def later(value, count):
        return jnp.where(spots >= count, pltpu.roll(value, count, 0), 0.0)

    def tap(f, back):
        return taps_ref[f, back : back + 1, :]

    def head(ref, before_ref, is_first):
        def before(f, back):
            value = before_ref[order + 4 + 2 * f + back - 1]
            return jnp.where(is_first, later(value, 1), value)

        key0 = ref[order] + tap(1, 1) * before(1, 1) + tap(1, 2) * before(1, 2)
        value0 = ref[order + 1] + tap(2, 1) * before(2, 1) + tap(2, 2) * before(2, 2)
        key1 = ref[order + 2] + tap(1, 2) * before(1, 1)
        value1 = ref[order + 3] + tap(2, 2) * before(2, 1)
        query0 = tap(0, 1) * before(0, 1) + tap(0, 2) * before(0, 2)
        query1 = tap(0, 2) * before(0, 1)
        return key0 * value0, key1 * value1, query0, query1

    gate0, gate1, query0, query1 = head(mine_ref, theirs_ref, first)
    their0, their1, _, _ = head(theirs_ref, mine_ref, jnp.logical_not(first))
    decay, states = [], []
    for n in range(order):
        rate = rates_ref[n : n + 1, :]
        factor0, factor1 = jnp.exp(-(length - 1) * rate), jnp.exp(-(length - 2) * rate)
        ours = mine_ref[n] + factor0 * gate0 + factor1 * gate1
        theirs = theirs_ref[n] + factor0 * their0 + factor1 * their1
        early, late = jnp.where(first, ours, theirs), jnp.where(first, theirs, ours)
        half = jnp.exp(-length * rate)
        total = half * early + late
        for count in (1, 2, 4):
            total = total + jnp.exp(-(2 * length * count) * rate) * later(total, count)
        before = later(total, 1)
        states.append(jnp.where(first, before, half * before + early))
        decay.append(jnp.broadcast_to(jnp.exp(-rate), (BLOCKS, LANES)))
    weights = [jnp.broadcast_to(weights_ref[n : n + 1, :], (BLOCKS, LANES)) for n in range(order)]
    skip = jnp.broadcast_to(skip_ref[...], (BLOCKS, LANES))

    def advance(r, states, gate, query):
        states = tuple(decay[n] * states[n] + gate for n in range(order))
        terms = [weights[n] * states[n] for n in range(order)] + [skip * gate]
        while len(terms) > 1:
            terms = [a + b for a, b in zip(terms[::2], terms[1::2])] + terms[len(terms) // 2 * 2 :]
        work[pl.ds(r, BLOCKS, stride=length), :] = query * terms[0]
        return states

    states = advance(0, tuple(states), gate0, every(query_ref, 0, length) + query0)
    states = advance(1, states, gate1, every(query_ref, 1, length) + query1)
    lax.fori_loop(
        2,
        length,
        lambda r, states: advance(r, states, every(gate_ref, r, length), every(query_ref, r, length)),
        states,
        unroll=6,
    )
    for place, (dy, dx) in enumerate(PLACES):
        spot = ((where_ref[3] + dy) & (Y - 1)) * XL + ((where_ref[4] + dx) & (XL - 1))
        there = pl.ds(pl.multiple_of(spot * length, length), length)
        out_ref[place * length : (place + 1) * length, :] = work[there, :].astype(BF)


def own_lanes(shape):
    return pl.BlockSpec(shape, lambda _, where_ref: (0,) * (len(shape) - 1) + (where_ref[5],))


def local_part(where, taps, rates, groups, blocks):
    tokens = sum(len(group) for group in blocks) * blocks_length(groups[0][0], blocks[0])
    flat = [term for terms in groups for term in terms]
    edges = (rates.shape[0] + 10, BLOCKS, LANES)
    tall = jax.ShapeDtypeStruct((tokens, LANES), F32)
    return pl.pallas_call(
        lambda *refs: local_kernel(blocks, [len(terms) for terms in groups], *refs),
        out_shape=(tall, tall, jax.ShapeDtypeStruct(edges, F32)),
        grid_spec=pltpu.PrefetchScalarGridSpec(
            num_scalar_prefetch=1,
            grid=(1,),
            in_specs=[own_lanes(taps.shape[:-1] + (LANES,)), own_lanes(rates.shape[:-1] + (LANES,))]
            + [whole(term.shape) for term in flat],
            out_specs=[whole(tall.shape), whole(tall.shape), whole(edges)],
            scratch_shapes=[pltpu.VMEM((tokens, LANES), F32)] * 5,
        ),
        name="local_part",
    )(where, taps, rates, *flat)


def blocks_length(term, group):
    return term.shape[0] // len(group)


def filtered(where, taps, rates, weights, skip, mine, theirs, query, gate):
    return pl.pallas_call(
        filter_kernel,
        out_shape=jax.ShapeDtypeStruct(gate.shape, BF),
        grid_spec=pltpu.PrefetchScalarGridSpec(
            num_scalar_prefetch=1,
            grid=(1,),
            in_specs=[own_lanes(array.shape[:-1] + (LANES,)) for array in (taps, rates, weights, skip)]
            + [whole(array.shape) for array in (mine, theirs, query, gate)],
            out_specs=whole(gate.shape),
            scratch_shapes=[pltpu.VMEM(gate.shape, F32)],
        ),
        name="filtered",
    )(where, taps, rates, weights, skip, mine, theirs, query, gate)


def body(activations, proj_weight, short_taps, residues, decay_rates, skip_gain, out_weight):
    tok_index = lax.axis_index("tok")
    ch_index = lax.axis_index("ch")
    z, xh, core = tok_index >> 2, (tok_index >> 1) & 1, tok_index & 1
    y, xl = ch_index >> 1, ch_index & 1
    where = jnp.stack([z, xh, core, y, xl, ch_index * (Z * XH) + (tok_index >> 1)]).astype(jnp.int32)
    length = activations.shape[0] // CORES

    kept = lax.dynamic_slice_in_dim(activations, core * length, length, 0)
    other = swap(lax.dynamic_slice_in_dim(activations, (1 - core) * length, length, 0))
    mine = jnp.concatenate([kept, other], axis=1)
    mine, proj_weight = lax.optimization_barrier((mine, proj_weight))

    def along(value, dy):
        return ch_send(value, ch_perm(lambda y, xl: (y - dy, xl)))

    def across(value):
        return ch_send(value, ch_perm(lambda y, xl: (y, 1 - xl)))

    blocks = [[(0, 0), (1, 0), (3, 0), (2, 0), (0, 1)], [(1, 1), (3, 1), (2, 1)]]
    first = [mine, along(mine, 1), along(mine, 3), along(mine, 2), across(mine)]
    half = len(TARGETS) // 2
    early, late = by_target(proj_weight, TARGETS[:half], TARGETS[half:])
    early, late = (early, swap(early)), (late, swap(late))
    first[4], first[1], first[2], early = lax.optimization_barrier((first[4], first[1], first[2], early))
    second = [along(first[4], 1), along(first[4], 3), across(first[3])]
    weights = list(zip(early, late))
    rows = jnp.concatenate(first)
    leaving = product(rows, weights, 0, 2), product(rows, weights, 2, 4)
    groups = reduce_groups(rows, leaving, jnp.concatenate(second), weights)
    groups, out_weight = lax.optimization_barrier((groups, out_weight))
    query, gate, edges = local_part(where, short_taps, decay_rates, groups, blocks)
    edges, out_weight = lax.optimization_barrier((edges, out_weight))
    their_edges = swap(edges)
    their_out = swap(out_weight)
    gated = filtered(where, short_taps, decay_rates, residues, skip_gain[None], edges, their_edges, query, gate)

    gated, their_out = lax.optimization_barrier((gated, their_out))
    out_rows = jnp.concatenate([out_weight, their_out], axis=1)

    pieces = {(0, 0): gated}
    pieces[0, 1] = tok_send(gated, X_SWAP)
    pieces[2, 0] = tok_send(gated, tok_perm(lambda z, xh, c: (z + 2, xh, c)))
    pieces[1, 0], pieces[3, 0] = tok_send(gated, Z_DOWN), tok_send(gated, Z_UP)
    pieces[1, 1], pieces[3, 1] = tok_send(pieces[0, 1], Z_DOWN), tok_send(pieces[0, 1], Z_UP)
    pieces[2, 1] = tok_send(pieces[2, 0], X_SWAP)
    gathered = jnp.zeros((gated.shape[0], Z * XH * LANES), BF)
    for (dz, dx), piece in pieces.items():
        chip = ((z + dz) & (Z - 1)) * XH + ((xh + dx) & (XH - 1))
        gathered = lax.dynamic_update_slice(gathered, piece, (0, chip * LANES))

    def part(first, last):
        rows = gathered[PLACES.index(first) * length : (PLACES.index(last) + 1) * length]
        return jnp.dot(rows, out_rows, preferred_element_type=F32)

    def forward(value, dy):
        return ch_send(value, ch_perm(lambda y, xl: (y + dy, xl)))

    far = across(part((2, 1), (2, 1)).astype(BF))
    up, down = [forward(part((dy, 1), (dy, 1)).astype(BF), dy) for dy in (1, 3)]
    far, *near = lax.optimization_barrier((far, part((1, 0), (1, 0)).astype(BF), part((3, 0), (3, 0)).astype(BF)))
    near_up, near_down = forward(near[0], 1), forward(near[1], 3)
    opposite = forward((part((2, 0), (2, 0)) + far.astype(F32)).astype(BF), 2)
    beside = across((part((0, 1), (0, 1)) + up.astype(F32) + down.astype(F32)).astype(BF))
    total = part((0, 0), (0, 0))
    for term in (near_up, near_down, opposite, beside):
        total = total + term.astype(F32)
    total = total.astype(BF)
    cols = out_weight.shape[1]
    kept, other = total[:, :cols], swap(total[:, cols:])
    return jnp.where(core == 0, jnp.concatenate([kept, other]), jnp.concatenate([other, kept]))


def solution(mesh):
    return jax.shard_map(
        body,
        mesh=mesh,
        in_specs=(P("ch", "tok"), P("tok", "ch"), P(), P(), P(), P(), P("ch", "tok")),
        out_specs=P("ch", "tok"),
        check_vma=False,
    )
```

```python
import jax
import jax.numpy as jnp
from jax import lax
from jax.experimental import pallas as pl
from jax.experimental.pallas import tpu as pltpu
from jax.sharding import PartitionSpec as P

Z, XH, CORES = 4, 2, 2
Y, XL = 4, 2
BLOCKS = Y * XL
LANES = 128
BF = jnp.bfloat16
F32 = jnp.float32


def tok_perm(move):
    pairs = []
    for z in range(Z):
        for xh in range(XH):
            for c in range(CORES):
                nz, nx, nc = move(z, xh, c)
                pairs.append(((z * XH + xh) * CORES + c, ((nz % Z) * XH + nx) * CORES + nc))
    return pairs


def ch_perm(move):
    pairs = []
    for y in range(Y):
        for xl in range(XL):
            ny, nx = move(y, xl)
            pairs.append((y * XL + xl, (ny % Y) * XL + nx))
    return pairs


CORE_SWAP = tok_perm(lambda z, xh, c: (z, xh, 1 - c))
Z_UP = tok_perm(lambda z, xh, c: (z + 1, xh, c))
Z_DOWN = tok_perm(lambda z, xh, c: (z - 1, xh, c))
X_SWAP = tok_perm(lambda z, xh, c: (z, 1 - xh, c))


def tok_send(value, perm):
    return lax.ppermute(value, "tok", perm)


def ch_send(value, perm):
    return lax.ppermute(value, "ch", perm)


def swap(value):
    return tok_send(value, CORE_SWAP)


def add(*terms):
    total = terms[0].astype(F32)
    for term in terms[1:]:
        total = total + term.astype(F32)
    return total.astype(BF)


def whole(shape):
    return pl.BlockSpec(shape, lambda *_: (0,) * len(shape))


PLACES = [(2, 1), (1, 0), (1, 1), (3, 0), (3, 1), (2, 0), (0, 1), (0, 0)]
TARGETS = [(2, 0), (1, 1), (2, 1), (3, 0), (1, 0), (0, 0), (0, 1), (3, 1)]


def reorder_kernel(parts, in_ref, *refs):
    out_refs, sems = refs[:-1], refs[-1]
    chip = lax.axis_index("tok") >> 1
    size = in_ref.shape[1] // len(TARGETS)
    copies = []
    for targets, out_ref in zip(parts, out_refs):
        for k, (dz, dx) in enumerate(targets):
            target = (((chip >> 1) + dz) & (Z - 1)) * XH + ((chip + dx) & (XH - 1))
            source = pl.ds(pl.multiple_of(target * size, size), size)
            place = pl.ds(k * size, size)
            sem = sems.at[len(copies)]
            copies.append(pltpu.make_async_copy(in_ref.at[:, source], out_ref.at[:, place], sem))
            copies[-1].start()
    for copy in copies:
        copy.wait()


def by_target(weight, *parts):
    width = weight.shape[1] // len(TARGETS)
    return pl.pallas_call(
        lambda *refs: reorder_kernel(parts, *refs),
        out_shape=[
            jax.ShapeDtypeStruct((weight.shape[0], width * len(targets)), weight.dtype) for targets in parts
        ],
        in_specs=[pl.BlockSpec(memory_space=pl.ANY)],
        out_specs=[pl.BlockSpec(memory_space=pltpu.VMEM)] * len(parts),
        scratch_shapes=[pltpu.SemaphoreType.DMA((sum(len(targets) for targets in parts),))],
        name="by_target",
    )(weight)


def product(rows, weights, first, last):
    own, other = weights
    depth, cols = own[0].shape
    each = len(TARGETS) // 2
    width = cols // each
    outs = []
    for part in range(len(own)):
        low, high = max(first - part * each, 0), min(last - part * each, each)
        if low < high:
            columns = slice(low * width, high * width)
            outs.append(
                jnp.dot(rows[:, :depth], own[part][:, columns], preferred_element_type=F32)
                + jnp.dot(rows[:, depth:], other[part][:, columns], preferred_element_type=F32)
            )
    return jnp.concatenate(outs, axis=1).astype(BF)


def split(value, count):
    width = value.shape[1] // count
    return [value[:, k * width : (k + 1) * width] for k in range(count)]


def reduce_groups(rows, leaving, late_rows, weights):
    up, down = tok_send(leaving[0], Z_UP), tok_send(leaving[1], Z_DOWN)
    rows, late_rows = lax.optimization_barrier((rows, late_rows))
    near_up, near, far, far_down = split(product(rows, weights, 4, 8), 4)

    far1, far2 = split(tok_send(product(late_rows, weights, 1, 3), X_SWAP), 2)
    far0, far3 = split(tok_send(product(late_rows, weights, 6, 8), X_SWAP), 2)
    near2 = product(late_rows, weights, 0, 1)
    near3 = product(late_rows, weights, 3, 4)
    near1, near0 = split(product(late_rows, weights, 4, 6), 2)
    near_in, far_in = split(up, 2)
    far_more, near_more = split(down, 2)
    far_down = tok_send(add(far_down, far_more), Z_DOWN)
    near_up = tok_send(add(near_up, near_in), Z_UP)
    near_up, far_down, near0, near1, near2, near3 = lax.optimization_barrier(
        (near_up, far_down, near0, near1, near2, near3)
    )
    crossed = tok_send(add(far, far_in, far_down), X_SWAP)
    terms = [add(near, near_more), near_up, crossed]

    half = late_rows.shape[0] // 2
    first, second = slice(0, half), slice(half, None)

    def both(near, far, side):
        return near[side].astype(F32) + far[side].astype(F32)

    up = tok_send(jnp.stack([both(near2, far2, first), both(near1, far1, second)]).astype(BF), Z_UP)
    down = tok_send(jnp.stack([both(near2, far2, second), both(near3, far3, first)]).astype(BF), Z_DOWN)
    from_below = tok_send((both(near1, far1, first) + up[0].astype(F32)).astype(BF), Z_UP)
    from_above = tok_send((both(near3, far3, second) + down[0].astype(F32)).astype(BF), Z_DOWN)
    late_terms = [
        jnp.concatenate(
            [
                both(near0, far0, first) + down[1].astype(F32) + from_below.astype(F32),
                both(near0, far0, second) + up[1].astype(F32) + from_above.astype(F32),
            ]
        ).astype(BF)
    ]
    return [terms, late_terms]


def features(block):
    half = LANES // 2
    low = lax.broadcasted_iota(jnp.int32, (1, LANES), 1) < half
    first, second, third = (block[:, k * LANES : (k + 1) * LANES] for k in range(3))
    return (
        jnp.where(low, first, second),
        jnp.where(low, pltpu.roll(first, half, 1), pltpu.roll(third, half, 1)),
        jnp.where(low, second, third),
    )


def every(ref, row, length):
    return ref[pl.ds(row, BLOCKS, stride=length), :]


def local_kernel(groups, counts, where_ref, taps_ref, rates_ref, *refs):
    flat = sum(counts)
    starts = [sum(counts[:g]) for g in range(len(counts))]
    term_refs = [refs[start : start + count] for start, count in zip(starts, counts)]
    query_ref, gate_ref, edge_ref = refs[flat : flat + 3]
    raw_refs = refs[flat + 3 : flat + 6]
    key_ref, value_ref, query_work, gate_work = refs[flat + 6 :]
    length = gate_ref.shape[0]
    order = rates_ref.shape[0]
    rows = lax.broadcasted_iota(jnp.int32, (length, LANES), 0)
    for refs_here, group in zip(term_refs, groups):
        for place, (dy, dx) in enumerate(group):
            here = slice(place * length, (place + 1) * length)
            block = refs_here[0][here, :].astype(F32)
            for ref in refs_here[1:]:
                block = block + ref[here, :].astype(F32)
            spot = ((where_ref[3] + dy) & (Y - 1)) * XL + ((where_ref[4] + dx) & (XL - 1))
            there = pl.ds(pl.multiple_of(spot * length, length), length)
            mixed = []
            for f, raw in enumerate(features(block)):
                raw_refs[f][there, :] = raw
                total = taps_ref[f, 0:1, :] * raw
                for back in (1, 2):
                    moved = jnp.where(rows >= back, pltpu.roll(raw, back, 0), 0.0)
                    total = total + taps_ref[f, back : back + 1, :] * moved
                mixed.append(total)
            query_work[spot] = mixed[0]
            key_ref[there, :] = mixed[1]
            value_ref[there, :] = mixed[2]
            gate_work[spot] = mixed[1] * mixed[2]
    gate_ref[...] = jnp.transpose(gate_work[...], (1, 0, 2))
    query_ref[...] = jnp.transpose(query_work[...], (1, 0, 2))
    decay = [
        jnp.broadcast_to(jnp.exp(-rates_ref[n : n + 1, :]), (BLOCKS, LANES)) for n in range(order)
    ]

    def step(r, states):
        gate = gate_ref[r]
        return tuple(decay[n] * states[n] + gate for n in range(order))

    states = lax.fori_loop(
        2, length, step, tuple(jnp.zeros((BLOCKS, LANES), F32) for _ in range(order)), unroll=14
    )
    for n in range(order):
        edge_ref[n] = states[n]
    at = order
    for r in (0, 1):
        edge_ref[at] = every(key_ref, r, length)
        edge_ref[at + 1] = every(value_ref, r, length)
        at += 2
    for f in range(3):
        for r in (length - 1, length - 2):
            edge_ref[at] = every(raw_refs[f], r, length)
            at += 1


def filter_kernel(where_ref, taps_ref, rates_ref, weights_ref, skip_ref, mine_ref, theirs_ref, query_ref, gate_ref, out_ref, work, turned):
    length = gate_ref.shape[0]
    order = rates_ref.shape[0]
    core = where_ref[2]
    first = core == 0
    spots = lax.broadcasted_iota(jnp.int32, (BLOCKS, LANES), 0)

    def later(value, count):
        return jnp.where(spots >= count, pltpu.roll(value, count, 0), 0.0)

    def tap(f, back):
        return taps_ref[f, back : back + 1, :]

    def head(ref, before_ref, is_first):
        def before(f, back):
            value = before_ref[order + 4 + 2 * f + back - 1]
            return jnp.where(is_first, later(value, 1), value)

        key0 = ref[order] + tap(1, 1) * before(1, 1) + tap(1, 2) * before(1, 2)
        value0 = ref[order + 1] + tap(2, 1) * before(2, 1) + tap(2, 2) * before(2, 2)
        key1 = ref[order + 2] + tap(1, 2) * before(1, 1)
        value1 = ref[order + 3] + tap(2, 2) * before(2, 1)
        query0 = tap(0, 1) * before(0, 1) + tap(0, 2) * before(0, 2)
        query1 = tap(0, 2) * before(0, 1)
        return key0 * value0, key1 * value1, query0, query1

    gate0, gate1, query0, query1 = head(mine_ref, theirs_ref, first)
    their0, their1, _, _ = head(theirs_ref, mine_ref, jnp.logical_not(first))
    decay, states = [], []
    for n in range(order):
        rate = rates_ref[n : n + 1, :]
        factor0, factor1 = jnp.exp(-(length - 1) * rate), jnp.exp(-(length - 2) * rate)
        ours = mine_ref[n] + factor0 * gate0 + factor1 * gate1
        theirs = theirs_ref[n] + factor0 * their0 + factor1 * their1
        early, late = jnp.where(first, ours, theirs), jnp.where(first, theirs, ours)
        half = jnp.exp(-length * rate)
        total = half * early + late
        for count in (1, 2, 4):
            total = total + jnp.exp(-(2 * length * count) * rate) * later(total, count)
        before = later(total, 1)
        states.append(jnp.where(first, before, half * before + early))
        decay.append(jnp.broadcast_to(jnp.exp(-rate), (BLOCKS, LANES)))
    weights = [jnp.broadcast_to(weights_ref[n : n + 1, :], (BLOCKS, LANES)) for n in range(order)]
    skip = jnp.broadcast_to(skip_ref[...], (BLOCKS, LANES))

    def advance(r, states, gate, query):
        states = tuple(decay[n] * states[n] + gate for n in range(order))
        terms = [weights[n] * states[n] for n in range(order)] + [skip * gate]
        while len(terms) > 1:
            terms = [a + b for a, b in zip(terms[::2], terms[1::2])] + terms[len(terms) // 2 * 2 :]
        work[r] = query * terms[0]
        return states

    states = advance(0, tuple(states), gate0, query_ref[0] + query0)
    states = advance(1, states, gate1, query_ref[1] + query1)
    lax.fori_loop(
        2,
        length,
        lambda r, states: advance(r, states, gate_ref[r], query_ref[r]),
        states,
        unroll=14,
    )
    turned[...] = jnp.transpose(work[...], (1, 0, 2))
    for place, (dy, dx) in enumerate(PLACES):
        spot = ((where_ref[3] + dy) & (Y - 1)) * XL + ((where_ref[4] + dx) & (XL - 1))
        out_ref[place * length : (place + 1) * length, :] = turned[spot].astype(BF)


def own_lanes(shape):
    return pl.BlockSpec(shape, lambda _, where_ref: (0,) * (len(shape) - 1) + (where_ref[5],))


def local_part(where, taps, rates, groups, blocks):
    tokens = sum(len(group) for group in blocks) * blocks_length(groups[0][0], blocks[0])
    flat = [term for terms in groups for term in terms]
    edges = (rates.shape[0] + 10, BLOCKS, LANES)
    tall = jax.ShapeDtypeStruct((tokens // BLOCKS, BLOCKS, LANES), F32)
    return pl.pallas_call(
        lambda *refs: local_kernel(blocks, [len(terms) for terms in groups], *refs),
        out_shape=(tall, tall, jax.ShapeDtypeStruct(edges, F32)),
        grid_spec=pltpu.PrefetchScalarGridSpec(
            num_scalar_prefetch=1,
            grid=(1,),
            in_specs=[own_lanes(taps.shape[:-1] + (LANES,)), own_lanes(rates.shape[:-1] + (LANES,))]
            + [whole(term.shape) for term in flat],
            out_specs=[whole(tall.shape), whole(tall.shape), whole(edges)],
            scratch_shapes=[pltpu.VMEM((tokens, LANES), F32)] * 5
            + [pltpu.VMEM((BLOCKS, tokens // BLOCKS, LANES), F32)] * 2,
        ),
        name="local_part",
    )(where, taps, rates, *flat)


def blocks_length(term, group):
    return term.shape[0] // len(group)


def filtered(where, taps, rates, weights, skip, mine, theirs, query, gate):
    return pl.pallas_call(
        filter_kernel,
        out_shape=jax.ShapeDtypeStruct((gate.shape[0] * BLOCKS, LANES), BF),
        grid_spec=pltpu.PrefetchScalarGridSpec(
            num_scalar_prefetch=1,
            grid=(1,),
            in_specs=[own_lanes(array.shape[:-1] + (LANES,)) for array in (taps, rates, weights, skip)]
            + [whole(array.shape) for array in (mine, theirs, query, gate)],
            out_specs=whole((gate.shape[0] * BLOCKS, LANES)),
            scratch_shapes=[pltpu.VMEM(gate.shape, F32), pltpu.VMEM((BLOCKS, gate.shape[0], LANES), F32)],
        ),
        name="filtered",
    )(where, taps, rates, weights, skip, mine, theirs, query, gate)


def body(activations, proj_weight, short_taps, residues, decay_rates, skip_gain, out_weight):
    tok_index = lax.axis_index("tok")
    ch_index = lax.axis_index("ch")
    z, xh, core = tok_index >> 2, (tok_index >> 1) & 1, tok_index & 1
    y, xl = ch_index >> 1, ch_index & 1
    where = jnp.stack([z, xh, core, y, xl, ch_index * (Z * XH) + (tok_index >> 1)]).astype(jnp.int32)
    length = activations.shape[0] // CORES

    kept = lax.dynamic_slice_in_dim(activations, core * length, length, 0)
    other = swap(lax.dynamic_slice_in_dim(activations, (1 - core) * length, length, 0))
    mine = jnp.concatenate([kept, other], axis=1)
    mine, proj_weight = lax.optimization_barrier((mine, proj_weight))

    def along(value, dy):
        return ch_send(value, ch_perm(lambda y, xl: (y - dy, xl)))

    def across(value):
        return ch_send(value, ch_perm(lambda y, xl: (y, 1 - xl)))

    blocks = [[(0, 0), (1, 0), (3, 0), (2, 0), (0, 1)], [(1, 1), (3, 1), (2, 1)]]
    first = [mine, along(mine, 1), along(mine, 3), along(mine, 2), across(mine)]
    half = len(TARGETS) // 2
    early, late = by_target(proj_weight, TARGETS[:half], TARGETS[half:])
    early, late = (early, swap(early)), (late, swap(late))
    first[4], first[1], first[2], early = lax.optimization_barrier((first[4], first[1], first[2], early))
    second = [along(first[4], 1), along(first[4], 3), across(first[3])]
    weights = list(zip(early, late))
    rows = jnp.concatenate(first)
    leaving = product(rows, weights, 0, 2), product(rows, weights, 2, 4)
    groups = reduce_groups(rows, leaving, jnp.concatenate(second), weights)
    groups, out_weight = lax.optimization_barrier((groups, out_weight))
    query, gate, edges = local_part(where, short_taps, decay_rates, groups, blocks)
    edges, out_weight = lax.optimization_barrier((edges, out_weight))
    their_edges = swap(edges)
    their_out = swap(out_weight)
    gated = filtered(where, short_taps, decay_rates, residues, skip_gain[None], edges, their_edges, query, gate)

    gated, their_out = lax.optimization_barrier((gated, their_out))
    out_rows = jnp.concatenate([out_weight, their_out], axis=1)

    pieces = {(0, 0): gated}
    pieces[0, 1] = tok_send(gated, X_SWAP)
    pieces[2, 0] = tok_send(gated, tok_perm(lambda z, xh, c: (z + 2, xh, c)))
    pieces[1, 0], pieces[3, 0] = tok_send(gated, Z_DOWN), tok_send(gated, Z_UP)
    pieces[1, 1], pieces[3, 1] = tok_send(pieces[0, 1], Z_DOWN), tok_send(pieces[0, 1], Z_UP)
    pieces[2, 1] = tok_send(pieces[2, 0], X_SWAP)
    gathered = jnp.zeros((gated.shape[0], Z * XH * LANES), BF)
    for (dz, dx), piece in pieces.items():
        chip = ((z + dz) & (Z - 1)) * XH + ((xh + dx) & (XH - 1))
        gathered = lax.dynamic_update_slice(gathered, piece, (0, chip * LANES))

    def part(first, last):
        rows = gathered[PLACES.index(first) * length : (PLACES.index(last) + 1) * length]
        return jnp.dot(rows, out_rows, preferred_element_type=F32)

    def forward(value, dy):
        return ch_send(value, ch_perm(lambda y, xl: (y + dy, xl)))

    far = across(part((2, 1), (2, 1)).astype(BF))
    up, down = [forward(part((dy, 1), (dy, 1)).astype(BF), dy) for dy in (1, 3)]
    far, *near = lax.optimization_barrier((far, part((1, 0), (1, 0)).astype(BF), part((3, 0), (3, 0)).astype(BF)))
    near_up, near_down = forward(near[0], 1), forward(near[1], 3)
    opposite = forward((part((2, 0), (2, 0)) + far.astype(F32)).astype(BF), 2)
    beside = across((part((0, 1), (0, 1)) + up.astype(F32) + down.astype(F32)).astype(BF))
    total = part((0, 0), (0, 0))
    for term in (near_up, near_down, opposite, beside):
        total = total + term.astype(F32)
    total = total.astype(BF)
    cols = out_weight.shape[1]
    kept, other = total[:, :cols], swap(total[:, cols:])
    return jnp.where(core == 0, jnp.concatenate([kept, other]), jnp.concatenate([other, kept]))


def solution(mesh):
    return jax.shard_map(
        body,
        mesh=mesh,
        in_specs=(P("ch", "tok"), P("tok", "ch"), P(), P(), P(), P(), P("ch", "tok")),
        out_specs=P("ch", "tok"),
        check_vma=False,
    )
```

```python
import jax
import jax.numpy as jnp
from jax import lax
from jax.experimental import pallas as pl
from jax.experimental.pallas import tpu as pltpu
from jax.sharding import PartitionSpec as P

Z, XH, CORES = 4, 2, 2
Y, XL = 4, 2
BLOCKS = Y * XL
LANES = 128
BF = jnp.bfloat16
F32 = jnp.float32


def tok_perm(move):
    pairs = []
    for z in range(Z):
        for xh in range(XH):
            for c in range(CORES):
                nz, nx, nc = move(z, xh, c)
                pairs.append(((z * XH + xh) * CORES + c, ((nz % Z) * XH + nx) * CORES + nc))
    return pairs


def ch_perm(move):
    pairs = []
    for y in range(Y):
        for xl in range(XL):
            ny, nx = move(y, xl)
            pairs.append((y * XL + xl, (ny % Y) * XL + nx))
    return pairs


CORE_SWAP = tok_perm(lambda z, xh, c: (z, xh, 1 - c))
Z_UP = tok_perm(lambda z, xh, c: (z + 1, xh, c))
Z_DOWN = tok_perm(lambda z, xh, c: (z - 1, xh, c))
X_SWAP = tok_perm(lambda z, xh, c: (z, 1 - xh, c))


def tok_send(value, perm):
    return lax.ppermute(value, "tok", perm)


def ch_send(value, perm):
    return lax.ppermute(value, "ch", perm)


def swap(value):
    return tok_send(value, CORE_SWAP)


def add(*terms):
    total = terms[0].astype(F32)
    for term in terms[1:]:
        total = total + term.astype(F32)
    return total.astype(BF)


def whole(shape):
    return pl.BlockSpec(shape, lambda *_: (0,) * len(shape))


PLACES = [(2, 1), (1, 0), (1, 1), (3, 0), (3, 1), (2, 0), (0, 1), (0, 0)]
TARGETS = [(2, 0), (1, 1), (2, 1), (3, 0), (1, 0), (0, 0), (0, 1), (3, 1)]


def reorder_kernel(parts, in_ref, *refs):
    out_refs, sems = refs[:-1], refs[-1]
    chip = lax.axis_index("tok") >> 1
    size = in_ref.shape[1] // len(TARGETS)
    copies = []
    for targets, out_ref in zip(parts, out_refs):
        for k, (dz, dx) in enumerate(targets):
            target = (((chip >> 1) + dz) & (Z - 1)) * XH + ((chip + dx) & (XH - 1))
            source = pl.ds(pl.multiple_of(target * size, size), size)
            place = pl.ds(k * size, size)
            sem = sems.at[len(copies)]
            copies.append(pltpu.make_async_copy(in_ref.at[:, source], out_ref.at[:, place], sem))
            copies[-1].start()
    for copy in copies:
        copy.wait()


def by_target(weight, *parts):
    width = weight.shape[1] // len(TARGETS)
    return pl.pallas_call(
        lambda *refs: reorder_kernel(parts, *refs),
        out_shape=[
            jax.ShapeDtypeStruct((weight.shape[0], width * len(targets)), weight.dtype) for targets in parts
        ],
        in_specs=[pl.BlockSpec(memory_space=pl.ANY)],
        out_specs=[pl.BlockSpec(memory_space=pltpu.VMEM)] * len(parts),
        scratch_shapes=[pltpu.SemaphoreType.DMA((sum(len(targets) for targets in parts),))],
        name="by_target",
    )(weight)


def product(rows, weights, first, last):
    own, other = weights
    depth, cols = own[0].shape
    each = len(TARGETS) // 2
    width = cols // each
    outs = []
    for part in range(len(own)):
        low, high = max(first - part * each, 0), min(last - part * each, each)
        if low < high:
            columns = slice(low * width, high * width)
            outs.append(
                jnp.dot(rows[:, :depth], own[part][:, columns], preferred_element_type=F32)
                + jnp.dot(rows[:, depth:], other[part][:, columns], preferred_element_type=F32)
            )
    return jnp.concatenate(outs, axis=1).astype(BF)


def split(value, count):
    width = value.shape[1] // count
    return [value[:, k * width : (k + 1) * width] for k in range(count)]


def reduce_groups(rows, leaving, late_rows, weights):
    up, down = tok_send(leaving[0], Z_UP), tok_send(leaving[1], Z_DOWN)
    rows, late_rows = lax.optimization_barrier((rows, late_rows))
    near_up, near, far, far_down = split(product(rows, weights, 4, 8), 4)

    far1, far2 = split(tok_send(product(late_rows, weights, 1, 3), X_SWAP), 2)
    far0, far3 = split(tok_send(product(late_rows, weights, 6, 8), X_SWAP), 2)
    near2 = product(late_rows, weights, 0, 1)
    near3 = product(late_rows, weights, 3, 4)
    near1, near0 = split(product(late_rows, weights, 4, 6), 2)
    near_in, far_in = split(up, 2)
    far_more, near_more = split(down, 2)
    far_down = tok_send(add(far_down, far_more), Z_DOWN)
    near_up = tok_send(add(near_up, near_in), Z_UP)
    near_up, far_down, near0, near1, near2, near3 = lax.optimization_barrier(
        (near_up, far_down, near0, near1, near2, near3)
    )
    crossed = tok_send(add(far, far_in, far_down), X_SWAP)
    terms = [add(near, near_more), near_up, crossed]

    half = late_rows.shape[0] // 2
    first, second = slice(0, half), slice(half, None)

    def both(near, far, side):
        return near[side].astype(F32) + far[side].astype(F32)

    up = tok_send(jnp.stack([both(near2, far2, first), both(near1, far1, second)]).astype(BF), Z_UP)
    down = tok_send(jnp.stack([both(near2, far2, second), both(near3, far3, first)]).astype(BF), Z_DOWN)
    from_below = tok_send((both(near1, far1, first) + up[0].astype(F32)).astype(BF), Z_UP)
    from_above = tok_send((both(near3, far3, second) + down[0].astype(F32)).astype(BF), Z_DOWN)
    late_terms = [
        (both(near0, far0, first) + down[1].astype(F32) + from_below.astype(F32)).astype(BF),
        (both(near0, far0, second) + up[1].astype(F32) + from_above.astype(F32)).astype(BF),
    ]
    return [terms, late_terms]


def features(block):
    half = LANES // 2
    low = lax.broadcasted_iota(jnp.int32, (1, LANES), 1) < half
    first, second, third = (block[:, k * LANES : (k + 1) * LANES] for k in range(3))
    return (
        jnp.where(low, first, second),
        jnp.where(low, pltpu.roll(first, half, 1), pltpu.roll(third, half, 1)),
        jnp.where(low, second, third),
    )


def every(ref, row, length):
    return ref[pl.ds(row, BLOCKS, stride=length), :]


def local_kernel(groups, counts, where_ref, taps_ref, rates_ref, *refs):
    flat = sum(counts)
    starts = [sum(counts[:g]) for g in range(len(counts))]
    term_refs = [refs[start : start + count] for start, count in zip(starts, counts)]
    query_ref, gate_ref, edge_ref = refs[flat : flat + 3]
    raw_refs = refs[flat + 3 : flat + 6]
    key_ref, value_ref, query_work, gate_work = refs[flat + 6 :]
    length = gate_ref.shape[0]
    order = rates_ref.shape[0]
    rows = lax.broadcasted_iota(jnp.int32, (length, LANES), 0)
    for refs_here, group in zip(term_refs, groups):
        for place, (dy, dx) in enumerate(group):
            here = slice(place * length, (place + 1) * length)
            if refs_here[0].shape[0] < len(group) * length:
                block = jnp.concatenate([ref[...] for ref in refs_here])[here].astype(F32)
            else:
                block = sum(ref[here, :].astype(F32) for ref in refs_here)
            spot = ((where_ref[3] + dy) & (Y - 1)) * XL + ((where_ref[4] + dx) & (XL - 1))
            there = pl.ds(pl.multiple_of(spot * length, length), length)
            mixed = []
            for f, raw in enumerate(features(block)):
                raw_refs[f][there, :] = raw
                total = taps_ref[f, 0:1, :] * raw
                for back in (1, 2):
                    moved = jnp.where(rows >= back, pltpu.roll(raw, back, 0), 0.0)
                    total = total + taps_ref[f, back : back + 1, :] * moved
                mixed.append(total)
            query_work[spot] = mixed[0]
            key_ref[there, :] = mixed[1]
            value_ref[there, :] = mixed[2]
            gate_work[spot] = mixed[1] * mixed[2]
    gate_ref[...] = jnp.transpose(gate_work[...], (1, 0, 2))
    query_ref[...] = jnp.transpose(query_work[...], (1, 0, 2))
    decay = [
        jnp.broadcast_to(jnp.exp(-rates_ref[n : n + 1, :]), (BLOCKS, LANES)) for n in range(order)
    ]

    def step(r, states):
        gate = gate_ref[r]
        return tuple(decay[n] * states[n] + gate for n in range(order))

    states = lax.fori_loop(
        2, length, step, tuple(jnp.zeros((BLOCKS, LANES), F32) for _ in range(order)), unroll=14
    )
    for n in range(order):
        edge_ref[n] = states[n]
    at = order
    for r in (0, 1):
        edge_ref[at] = every(key_ref, r, length)
        edge_ref[at + 1] = every(value_ref, r, length)
        at += 2
    for f in range(3):
        for r in (length - 1, length - 2):
            edge_ref[at] = every(raw_refs[f], r, length)
            at += 1


def filter_kernel(where_ref, taps_ref, rates_ref, weights_ref, skip_ref, mine_ref, theirs_ref, query_ref, gate_ref, out_ref, work, turned):
    length = gate_ref.shape[0]
    order = rates_ref.shape[0]
    core = where_ref[2]
    first = core == 0
    spots = lax.broadcasted_iota(jnp.int32, (BLOCKS, LANES), 0)

    def later(value, count):
        return jnp.where(spots >= count, pltpu.roll(value, count, 0), 0.0)

    def tap(f, back):
        return taps_ref[f, back : back + 1, :]

    def head(ref, before_ref, is_first):
        def before(f, back):
            value = before_ref[order + 4 + 2 * f + back - 1]
            return jnp.where(is_first, later(value, 1), value)

        key0 = ref[order] + tap(1, 1) * before(1, 1) + tap(1, 2) * before(1, 2)
        value0 = ref[order + 1] + tap(2, 1) * before(2, 1) + tap(2, 2) * before(2, 2)
        key1 = ref[order + 2] + tap(1, 2) * before(1, 1)
        value1 = ref[order + 3] + tap(2, 2) * before(2, 1)
        query0 = tap(0, 1) * before(0, 1) + tap(0, 2) * before(0, 2)
        query1 = tap(0, 2) * before(0, 1)
        return key0 * value0, key1 * value1, query0, query1

    gate0, gate1, query0, query1 = head(mine_ref, theirs_ref, first)
    their0, their1, _, _ = head(theirs_ref, mine_ref, jnp.logical_not(first))
    decay, states = [], []
    for n in range(order):
        rate = rates_ref[n : n + 1, :]
        factor0, factor1 = jnp.exp(-(length - 1) * rate), jnp.exp(-(length - 2) * rate)
        ours = mine_ref[n] + factor0 * gate0 + factor1 * gate1
        theirs = theirs_ref[n] + factor0 * their0 + factor1 * their1
        early, late = jnp.where(first, ours, theirs), jnp.where(first, theirs, ours)
        half = jnp.exp(-length * rate)
        total = half * early + late
        for count in (1, 2, 4):
            total = total + jnp.exp(-(2 * length * count) * rate) * later(total, count)
        before = later(total, 1)
        states.append(jnp.where(first, before, half * before + early))
        decay.append(jnp.broadcast_to(jnp.exp(-rate), (BLOCKS, LANES)))
    weights = [jnp.broadcast_to(weights_ref[n : n + 1, :], (BLOCKS, LANES)) for n in range(order)]
    skip = jnp.broadcast_to(skip_ref[...], (BLOCKS, LANES))

    def advance(r, states, gate, query):
        states = tuple(decay[n] * states[n] + gate for n in range(order))
        terms = [weights[n] * states[n] for n in range(order)] + [skip * gate]
        while len(terms) > 1:
            terms = [a + b for a, b in zip(terms[::2], terms[1::2])] + terms[len(terms) // 2 * 2 :]
        work[r] = query * terms[0]
        return states

    states = advance(0, tuple(states), gate0, query_ref[0] + query0)
    states = advance(1, states, gate1, query_ref[1] + query1)
    lax.fori_loop(
        2,
        length,
        lambda r, states: advance(r, states, gate_ref[r], query_ref[r]),
        states,
        unroll=14,
    )
    turned[...] = jnp.transpose(work[...], (1, 0, 2))
    for place, (dy, dx) in enumerate(PLACES):
        spot = ((where_ref[3] + dy) & (Y - 1)) * XL + ((where_ref[4] + dx) & (XL - 1))
        out_ref[place * length : (place + 1) * length, :] = turned[spot].astype(BF)


def own_lanes(shape):
    return pl.BlockSpec(shape, lambda _, where_ref: (0,) * (len(shape) - 1) + (where_ref[5],))


def local_part(where, taps, rates, groups, blocks):
    tokens = sum(len(group) for group in blocks) * blocks_length(groups[0][0], blocks[0])
    flat = [term for terms in groups for term in terms]
    edges = (rates.shape[0] + 10, BLOCKS, LANES)
    tall = jax.ShapeDtypeStruct((tokens // BLOCKS, BLOCKS, LANES), F32)
    return pl.pallas_call(
        lambda *refs: local_kernel(blocks, [len(terms) for terms in groups], *refs),
        out_shape=(tall, tall, jax.ShapeDtypeStruct(edges, F32)),
        grid_spec=pltpu.PrefetchScalarGridSpec(
            num_scalar_prefetch=1,
            grid=(1,),
            in_specs=[own_lanes(taps.shape[:-1] + (LANES,)), own_lanes(rates.shape[:-1] + (LANES,))]
            + [whole(term.shape) for term in flat],
            out_specs=[whole(tall.shape), whole(tall.shape), whole(edges)],
            scratch_shapes=[pltpu.VMEM((tokens, LANES), F32)] * 5
            + [pltpu.VMEM((BLOCKS, tokens // BLOCKS, LANES), F32)] * 2,
        ),
        name="local_part",
    )(where, taps, rates, *flat)


def blocks_length(term, group):
    return term.shape[0] // len(group)


def filtered(where, taps, rates, weights, skip, mine, theirs, query, gate):
    return pl.pallas_call(
        filter_kernel,
        out_shape=jax.ShapeDtypeStruct((gate.shape[0] * BLOCKS, LANES), BF),
        grid_spec=pltpu.PrefetchScalarGridSpec(
            num_scalar_prefetch=1,
            grid=(1,),
            in_specs=[own_lanes(array.shape[:-1] + (LANES,)) for array in (taps, rates, weights, skip)]
            + [whole(array.shape) for array in (mine, theirs, query, gate)],
            out_specs=whole((gate.shape[0] * BLOCKS, LANES)),
            scratch_shapes=[pltpu.VMEM(gate.shape, F32), pltpu.VMEM((BLOCKS, gate.shape[0], LANES), F32)],
        ),
        name="filtered",
    )(where, taps, rates, weights, skip, mine, theirs, query, gate)


def body(activations, proj_weight, short_taps, residues, decay_rates, skip_gain, out_weight):
    tok_index = lax.axis_index("tok")
    ch_index = lax.axis_index("ch")
    z, xh, core = tok_index >> 2, (tok_index >> 1) & 1, tok_index & 1
    y, xl = ch_index >> 1, ch_index & 1
    where = jnp.stack([z, xh, core, y, xl, ch_index * (Z * XH) + (tok_index >> 1)]).astype(jnp.int32)
    length = activations.shape[0] // CORES

    kept = lax.dynamic_slice_in_dim(activations, core * length, length, 0)
    other = swap(lax.dynamic_slice_in_dim(activations, (1 - core) * length, length, 0))
    mine = jnp.concatenate([kept, other], axis=1)
    mine, proj_weight = lax.optimization_barrier((mine, proj_weight))

    def along(value, dy):
        return ch_send(value, ch_perm(lambda y, xl: (y - dy, xl)))

    def across(value):
        return ch_send(value, ch_perm(lambda y, xl: (y, 1 - xl)))

    blocks = [[(0, 0), (1, 0), (3, 0), (2, 0), (0, 1)], [(1, 1), (3, 1), (2, 1)]]
    first = [mine, along(mine, 1), along(mine, 3), along(mine, 2), across(mine)]
    half = len(TARGETS) // 2
    early, late = by_target(proj_weight, TARGETS[:half], TARGETS[half:])
    early, late = (early, swap(early)), (late, swap(late))
    first[4], first[1], first[2], early = lax.optimization_barrier((first[4], first[1], first[2], early))
    second = [along(first[4], 1), along(first[4], 3), across(first[3])]
    weights = list(zip(early, late))
    rows = jnp.concatenate(first)
    leaving = product(rows, weights, 0, 2), product(rows, weights, 2, 4)
    groups = reduce_groups(rows, leaving, jnp.concatenate(second), weights)
    groups, out_weight = lax.optimization_barrier((groups, out_weight))
    query, gate, edges = local_part(where, short_taps, decay_rates, groups, blocks)
    edges, out_weight = lax.optimization_barrier((edges, out_weight))
    their_edges = swap(edges)
    their_out = swap(out_weight)
    gated = filtered(where, short_taps, decay_rates, residues, skip_gain[None], edges, their_edges, query, gate)

    gated, their_out = lax.optimization_barrier((gated, their_out))
    out_rows = jnp.concatenate([out_weight, their_out], axis=1)

    pieces = {(0, 0): gated}
    pieces[0, 1] = tok_send(gated, X_SWAP)
    pieces[2, 0] = tok_send(gated, tok_perm(lambda z, xh, c: (z + 2, xh, c)))
    pieces[1, 0], pieces[3, 0] = tok_send(gated, Z_DOWN), tok_send(gated, Z_UP)
    pieces[1, 1], pieces[3, 1] = tok_send(pieces[0, 1], Z_DOWN), tok_send(pieces[0, 1], Z_UP)
    pieces[2, 1] = tok_send(pieces[2, 0], X_SWAP)
    gathered = jnp.zeros((gated.shape[0], Z * XH * LANES), BF)
    for (dz, dx), piece in pieces.items():
        chip = ((z + dz) & (Z - 1)) * XH + ((xh + dx) & (XH - 1))
        gathered = lax.dynamic_update_slice(gathered, piece, (0, chip * LANES))

    def part(first, last):
        rows = gathered[PLACES.index(first) * length : (PLACES.index(last) + 1) * length]
        return jnp.dot(rows, out_rows, preferred_element_type=F32)

    def forward(value, dy):
        return ch_send(value, ch_perm(lambda y, xl: (y + dy, xl)))

    far = across(part((2, 1), (2, 1)).astype(BF))
    up, down = [forward(part((dy, 1), (dy, 1)).astype(BF), dy) for dy in (1, 3)]
    far, *near = lax.optimization_barrier((far, part((1, 0), (1, 0)).astype(BF), part((3, 0), (3, 0)).astype(BF)))
    near_up, near_down = forward(near[0], 1), forward(near[1], 3)
    opposite = forward((part((2, 0), (2, 0)) + far.astype(F32)).astype(BF), 2)
    beside = across((part((0, 1), (0, 1)) + up.astype(F32) + down.astype(F32)).astype(BF))
    total = part((0, 0), (0, 0))
    for term in (near_up, near_down, opposite, beside):
        total = total + term.astype(F32)
    total = total.astype(BF)
    cols = out_weight.shape[1]
    kept, other = total[:, :cols], swap(total[:, cols:])
    return jnp.where(core == 0, jnp.concatenate([kept, other]), jnp.concatenate([other, kept]))


def solution(mesh):
    return jax.shard_map(
        body,
        mesh=mesh,
        in_specs=(P("ch", "tok"), P("tok", "ch"), P(), P(), P(), P(), P("ch", "tok")),
        out_specs=P("ch", "tok"),
        check_vma=False,
    )
```
